32 devices in a mesh: gx: 4 (over y, x), gy: 8 (over z, core).
Axes of the slice: x: 2, y: 2, z: 4, core: 2. Of those that a mesh axis runs over, the one named last changes fastest.
Arguments:
- stream: bfloat16 [768, 4096], P('gy', 'gx'), may hold values from -40 to 40
- qkv_weight: bfloat16 [4096, 12288], P('gx', 'gy'), may hold values from -0.1875 to 0.1875
- up_weight: bfloat16 [4096, 16384], P('gx', 'gy'), may hold values from -0.09375 to 0.09375
- out_weight: bfloat16 [4096, 4096], P('gy', 'gx'), may hold values from -0.09375 to 0.09375
- down_weight: bfloat16 [16384, 4096], P('gy', 'gx'), may hold values from -0.046875 to 0.046875
- cache_keys: bfloat16 [896, 4096], P('gx', 'gy'), may hold values from -400 to 400
- cache_values: bfloat16 [896, 4096], P('gx', 'gy'), may hold values from -12 to 12
- request_prefix: int32 [6], replicated, may hold values from 0 to 1
- request_lengths: int32 [6], replicated, may hold values from 1 to 192, 768 in all
- owner_list: int32 [4], replicated, may hold values from 0 to 3, each once
Outputs:
- layer_out: float32 [768, 4096], P('gy', 'gx')
The draws below stay inside these ranges and needn't reach their ends.
Inputs may be any that keep to these rules, and one draw needn't show every extreme that they name: `request_lengths`: they sum to 768, and the largest is exactly 192. `owner_list`: each of 0 to 3 appears once.
All inputs are finite; a program needn't handle non-finite values.
Results may differ from the reference program's by a relative error of at most 0.0084.
Values may be sent and summed in bfloat16 or wider, within the bound.
No kernel may reach another device: no remote copies, remote signals or barrier semaphores. Data moves between devices by JAX's collectives and lax.ppermute only.
A program may use at most 128 MiB of HBM per device.

```python
import math
import jax
import jax.numpy as jnp
import numpy as np
from jax import lax

D = 4096
HEADS = 32
HD = 128
FF = 16384
ROT = 32
SUF_TOK = 768
BLK = 224
REQ = 6
MOST_LEN = 192
PLEN = 448
KEYS_ALL = 896
N_GX = 4


def draw_stream(key, part):
    key_main = jax.random.fold_in(key, 11)
    key_cols = jax.random.fold_in(key, 12)
    key_rows = jax.random.fold_in(key, 13)
    column = jnp.arange(D, dtype=jnp.float32) / D
    col_scale = 10.0 ** (column - 0.5) * jnp.exp(jax.random.uniform(key_cols, (D,), jnp.float32, -0.3, 0.3))
    row_scale = 10.0 ** jax.random.uniform(key_rows, (SUF_TOK, 1), jnp.float32, -0.5, 0.5)
    result = row_scale * jax.random.normal(key_main, (SUF_TOK, D), jnp.float32) * col_scale[None, :]
    return jnp.clip(result, -40.0, 40.0).astype(jnp.bfloat16)


def draw_cache_keys(key, part):
    key_main = jax.random.fold_in(key, 21)
    result = jax.random.normal(key_main, (KEYS_ALL, D), jnp.float32) * 1.5
    return jnp.clip(result, -400.0, 400.0).astype(jnp.bfloat16)


def plant(values, own_key, least, top_value):
    spot = [jax.random.randint(jax.random.fold_in(own_key, axis), (), 0, length) for axis, length in enumerate(values.shape)]
    widest = values.shape.index(max(values.shape))
    neighbour = spot[:widest] + [(spot[widest] + 1) % values.shape[widest]] + spot[widest + 1:]
    return values.at[tuple(spot)].set(least).at[tuple(neighbour)].set(top_value)


def steps_of(rng, extent, split, least, high):
    level, own = 1.0, jax.random.fold_in(rng, 6)
    for dim, parts in split:
        draws = jnp.exp(jax.random.uniform(jax.random.fold_in(own, dim), (parts,), jnp.float32, least / len(split), high / len(split)))
        level = level * jnp.repeat(draws, extent[dim] // parts).reshape([-1 if axis == dim else 1 for axis in range(len(extent))])
    return level


def length_profile(amount, total, limit, slope):
    loads = [(1 << 20) // math.isqrt(rank ** slope) + 1 for rank in range(2, amount + 1)]
    spare, holding = total - limit - (amount - 1), [1] * (amount - 1)
    while spare > 0:
        movable = [i for i in range(amount - 1) if holding[i] < limit]
        pool, remaining = sum([loads[i] for i in movable]), spare
        for i in movable:
            addition = min(limit - holding[i], max(1, remaining * loads[i] // pool), spare)
            holding[i] = holding[i] + addition
            spare = spare - addition
    return np.array([limit] + holding)


def uneven(stream_key, count, total, reach, skew):
    if count == 2:
        one = jax.random.randint(stream_key, (), max(1, total - reach), min(reach, total - 1) + 1)
        return jnp.stack([one, total - one])
    sizes = jnp.asarray(length_profile(count, total, reach, skew), jnp.int32)
    pairs = (count - 1) // 2
    giver, receiver = sizes[1:1 + 2 * pairs:2], sizes[2:2 + 2 * pairs:2]
    slack = jnp.minimum(giver - 1, reach - receiver)
    shifted = jax.random.randint(jax.random.fold_in(stream_key, 1), (pairs,), 0, 1 << 20) % (slack + 1)
    sizes = sizes.at[1:1 + 2 * pairs:2].set(giver - shifted).at[2:2 + 2 * pairs:2].set(receiver + shifted)
    return sizes[jax.random.permutation(jax.random.fold_in(stream_key, 2), count)]


def centred(rng, dims, width, reach, cuts=(), kind=jnp.bfloat16):
    values = jax.random.normal(rng, dims, jnp.float32) * width
    if len(cuts) > 0:
        values = steps_of(rng, dims, cuts, -0.22, 0.18) * values
    return jnp.clip(values, min=-reach, max=reach).astype(kind)


def setup_inputs(seed: int = 0) -> dict:
    splits = jax.random.split(jax.random.key(seed), 11)
    return {
        "stream": draw_stream(jax.random.fold_in(splits[10], 71), 0),
        "qkv_weight": centred(splits[1], (D, 3 * D), (D // 4) ** -0.5, 0.1875, ((0, 4), (1, 8))),
        "up_weight": centred(splits[2], (D, FF), D ** -0.5, 0.09375, ((0, 4), (1, 8))),
        "out_weight": centred(splits[3], (D, D), D ** -0.5, 0.09375, ((0, 8), (1, 4))),
        "down_weight": centred(splits[4], (FF, D), FF ** -0.5, 0.046875, ((0, 8), (1, 4))),
        "cache_keys": draw_cache_keys(jax.random.fold_in(splits[10], 71), 0),
        "cache_values": centred(splits[6], (KEYS_ALL, D), 2.0, 12.0, ((0, 4), (1, 8))),
        "request_prefix": plant(jax.random.randint(splits[7], (REQ,), 0, 2), jax.random.fold_in(splits[7], 1), 0, 1).astype(jnp.int32),
        "request_lengths": uneven(splits[8], REQ, SUF_TOK, MOST_LEN, 1).astype(jnp.int32),
        "owner_list": jax.random.permutation(splits[9], N_GX).astype(jnp.int32),
    }


epsilon = 1e-05
rotary_base = 10000.0

def token_layout(request_lengths, token_count):
    ending = jnp.cumsum(request_lengths).astype(jnp.int32)
    starting = (ending - request_lengths).astype(jnp.int32)
    token_ids = jnp.arange(token_count, dtype=jnp.int32)
    segment = lax.optimization_barrier(jnp.sum((token_ids[:, None] >= ending[None, :]).astype(jnp.int32), axis=1)).astype(jnp.int32)
    member = segment[:, None] == jnp.arange(request_lengths.shape[0], dtype=jnp.int32)[None, :]
    first_token = lax.optimization_barrier(jnp.sum(jnp.where(member, starting[None, :], 0), axis=1)).astype(jnp.int32)
    return (token_ids, segment, (token_ids - first_token).astype(jnp.int32), member)

def rotate(vectors, angle_pos):
    halfway = ROT // 2
    frequency = rotary_base ** (-2.0 * jnp.arange(halfway, dtype=jnp.float32) / ROT)
    angles = angle_pos[:, None] * frequency[None, :]
    cosine = jnp.cos(angles)[:, None, :]
    sine_part = jnp.sin(angles)[:, None, :]
    leading = vectors[..., :halfway]
    trailing = vectors[..., halfway:ROT]
    return jnp.concatenate([leading * cosine - trailing * sine_part, trailing * cosine + leading * sine_part, vectors[..., ROT:]], axis=-1)

def reference(stream, qkv_weight, up_weight, out_weight, down_weight, cache_keys, cache_values, request_prefix, request_lengths, owner_list):
    token_count = stream.shape[0]
    values32 = stream.astype(jnp.float32)
    average = lax.optimization_barrier(jnp.mean(values32, axis=1, keepdims=True))
    square = lax.optimization_barrier(jnp.mean(values32 * values32, axis=1, keepdims=True))
    normed = ((values32 - average) * lax.rsqrt(square - average * average + epsilon)).astype(jnp.bfloat16)
    projected = jnp.dot(normed, qkv_weight, preferred_element_type=jnp.float32).reshape(token_count, HEADS, 3, HD)
    up_sums = jnp.dot(normed, up_weight, preferred_element_type=jnp.float32)
    hidden = jax.nn.gelu(up_sums, approximate=False).astype(jnp.bfloat16)
    token_ids, segment, offsets, member = token_layout(request_lengths, token_count)
    angle_pos = (offsets + PLEN).astype(jnp.float32)
    queries = rotate(projected[:, :, 0], angle_pos).astype(jnp.bfloat16)
    keys_new = rotate(projected[:, :, 1], angle_pos).astype(jnp.bfloat16)
    values_new = projected[:, :, 2].astype(jnp.bfloat16)
    halfway = N_GX // 2
    slot_index = jnp.arange(N_GX, dtype=jnp.int32)
    upper_half = (slot_index >= halfway).astype(jnp.int32)
    block_prefix = lax.optimization_barrier(jnp.sum(jnp.where(owner_list[None, :] == slot_index[:, None], upper_half[None, :], 0), axis=1)).astype(jnp.int32)
    token_prefix = lax.optimization_barrier(jnp.sum(jnp.where(member, request_prefix[None, :], 0), axis=1)).astype(jnp.int32)
    key_prefix = jnp.repeat(block_prefix, BLK)
    cache_allowed = token_prefix[:, None] == key_prefix[None, :]
    own_allowed = (segment[:, None] == segment[None, :]) & (token_ids[None, :] <= token_ids[:, None])
    score_scale = HD ** (-0.5)

    def one_head(operands):
        head_query, head_keys, head_values, old_keys, old_values = operands
        cached = jnp.dot(head_query, old_keys.T, preferred_element_type=jnp.float32) * score_scale
        cached = jnp.where(cache_allowed, cached, -jnp.inf)
        recent = jnp.dot(head_query, head_keys.T, preferred_element_type=jnp.float32) * score_scale
        recent = jnp.where(own_allowed, recent, -jnp.inf)
        largest = jnp.maximum(lax.optimization_barrier(jnp.max(cached, axis=1)), lax.optimization_barrier(jnp.max(recent, axis=1)))[:, None]
        cached_weights = jnp.exp(cached - largest)
        recent_weights = jnp.exp(recent - largest)
        totals = lax.optimization_barrier(jnp.sum(cached_weights, axis=1)) + lax.optimization_barrier(jnp.sum(recent_weights, axis=1))
        summed = jnp.dot(cached_weights.astype(jnp.bfloat16), old_values, preferred_element_type=jnp.float32)
        summed = summed + jnp.dot(recent_weights.astype(jnp.bfloat16), head_values, preferred_element_type=jnp.float32)
        return summed / totals[:, None]
    operands = (jnp.transpose(queries, (1, 0, 2)), jnp.transpose(keys_new, (1, 0, 2)), jnp.transpose(values_new, (1, 0, 2)), jnp.transpose(cache_keys.reshape(KEYS_ALL, HEADS, HD), (1, 0, 2)), jnp.transpose(cache_values.reshape(KEYS_ALL, HEADS, HD), (1, 0, 2)))
    heads_out = lax.map(one_head, operands)
    context = jnp.transpose(heads_out, (1, 0, 2)).reshape(token_count, D).astype(jnp.bfloat16)
    mixed_sum = jnp.dot(context, out_weight, preferred_element_type=jnp.float32) + jnp.dot(hidden, down_weight, preferred_element_type=jnp.float32)
    return values32 + mixed_sum
```

```python
import functools

import jax
import jax.numpy as jnp
from jax import lax
from jax.experimental import pallas as pl
from jax.experimental.pallas import tpu as pltpu
from jax.sharding import PartitionSpec as P

HD = 128
ROT = 32


epsilon = 1e-05
rotary_base = 10000.0
masked_score = -1e30


def token_layout(request_lengths, token_count):
    ending = jnp.cumsum(request_lengths)
    starting = ending - request_lengths
    token_ids = jnp.arange(token_count, dtype=jnp.int32)
    segment = jnp.sum((token_ids[:, None] >= ending[None, :]).astype(jnp.int32), axis=1)
    member = segment[:, None] == jnp.arange(request_lengths.shape[0], dtype=jnp.int32)[None, :]
    first_token = jnp.sum(jnp.where(member, starting[None, :], 0), axis=1)
    return (token_ids, segment, token_ids - first_token, member)


def rotate(vectors, angle_pos):
    halfway = ROT // 2
    frequency = rotary_base ** (-2.0 * jnp.arange(halfway, dtype=jnp.float32) / ROT)
    angles = angle_pos[:, None] * frequency[None, :]
    cosine = jnp.cos(angles)[:, None, :]
    sine_part = jnp.sin(angles)[:, None, :]
    leading = vectors[..., :halfway]
    trailing = vectors[..., halfway:ROT]
    return jnp.concatenate(
        [
            leading * cosine - trailing * sine_part,
            trailing * cosine + leading * sine_part,
            vectors[..., ROT:],
        ],
        axis=-1,
    )


def split_heads(head_block, angle_pos, head_count):
    rows_here = head_block.shape[0]
    head_parts = head_block.reshape(rows_here, head_count, 3, HD)
    queries = rotate(head_parts[:, :, 0], angle_pos).astype(jnp.bfloat16)
    keys_new = rotate(head_parts[:, :, 1], angle_pos).astype(jnp.bfloat16)
    values_new = head_parts[:, :, 2].astype(jnp.bfloat16)
    return (queries, keys_new, values_new)


def shards(
    stream,
    qkv_weight,
    up_weight,
    out_weight,
    down_weight,
    cache_keys,
    cache_values,
    request_prefix,
    request_lengths,
    owner_list,
):
    groups = lax.axis_size("gx")
    group_index = lax.axis_index("gx")
    local_rows = stream.shape[0]
    feature_count = stream.shape[1] * groups
    token_count = local_rows * lax.axis_size("gy")
    share_rows = token_count // groups
    head_cols = qkv_weight.shape[1]
    head_count = head_cols // (3 * HD)
    block_len = cache_keys.shape[0]
    prefix_len = block_len * groups // 2
    score_scale = HD ** (-0.5)
    values32 = stream.astype(jnp.float32)
    moments = lax.psum((jnp.sum(values32, axis=1), jnp.sum(values32 * values32, axis=1)), "gx")
    average = (moments[0] / feature_count)[:, None]
    square = (moments[1] / feature_count)[:, None]
    normed = ((values32 - average) * lax.rsqrt(square - average * average + epsilon)).astype(
        jnp.bfloat16
    )
    row_piece = lax.all_gather(normed, "gy", axis=0, tiled=True)
    partial_sums = jnp.concatenate(
        [
            jnp.dot(row_piece, qkv_weight, preferred_element_type=jnp.float32),
            jnp.dot(row_piece, up_weight, preferred_element_type=jnp.float32),
        ],
        axis=1,
    )
    token_ids, segment, offsets, member = token_layout(request_lengths, token_count)
    angle_pos = (offsets + prefix_len).astype(jnp.float32)
    first_row = group_index * share_rows
    summed = lax.psum_scatter(partial_sums, "gx", scatter_dimension=0, tiled=True)
    up_own = summed[:, head_cols:]
    own_angles = lax.dynamic_slice_in_dim(angle_pos, first_row, share_rows)
    own_query, own_keys, own_values = split_heads(summed[:, :head_cols], own_angles, head_count)
    queries, keys_new, values_new = (
        lax.all_gather(own_query, "gx", axis=0, tiled=True),
        lax.all_gather(own_keys, "gx", axis=0, tiled=True),
        lax.all_gather(own_values, "gx", axis=0, tiled=True),
    )
    hidden_own = jax.nn.gelu(up_own, approximate=False).astype(jnp.bfloat16)
    mine_query = lax.dynamic_slice_in_dim(queries, first_row, share_rows)
    mine_ids = lax.dynamic_slice_in_dim(token_ids, first_row, share_rows)
    mine_segment = lax.dynamic_slice_in_dim(segment, first_row, share_rows)
    visible = (mine_segment[:, None] == segment[None, :]) & (
        token_ids[None, :] <= mine_ids[:, None]
    )
    recent = (
        jnp.einsum("qhd,khd->hqk", mine_query, keys_new, preferred_element_type=jnp.float32)
        * score_scale
    )
    recent = jnp.where(visible[None], recent, masked_score)
    recent_peak = jnp.max(recent, axis=2)
    recent_weights = jnp.exp(recent - recent_peak[..., None])
    recent_total = jnp.sum(recent_weights, axis=2)
    recent_out = jnp.einsum(
        "hqk,khd->hqd",
        recent_weights.astype(jnp.bfloat16),
        values_new,
        preferred_element_type=jnp.float32,
    )
    halfway = groups // 2
    slot_index = jnp.arange(groups, dtype=jnp.int32)
    held_prefix = jnp.sum(
        jnp.where(owner_list == group_index, (slot_index >= halfway).astype(jnp.int32), 0)
    )
    token_prefix = jnp.sum(jnp.where(member, request_prefix[None, :], 0), axis=1)
    active = (token_prefix == held_prefix)[None, :, None]
    step_len = min(512, block_len)
    key_blocks = cache_keys.reshape(block_len // step_len, step_len, head_count, HD)
    value_blocks = cache_values.reshape(block_len // step_len, step_len, head_count, HD)

    def visit(carried, blocks):
        run_peak, run_total, run_out = carried
        block_keys, block_values = blocks
        scores = (
            jnp.einsum("qhd,khd->hqk", queries, block_keys, preferred_element_type=jnp.float32)
            * score_scale
        )
        scores = jnp.where(active, scores, masked_score)
        new_peak = jnp.maximum(run_peak, jnp.max(scores, axis=2))
        fading = jnp.exp(run_peak - new_peak)
        weights = jnp.exp(scores - new_peak[..., None])
        run_total = run_total * fading + jnp.sum(weights, axis=2)
        run_out = run_out * fading[..., None] + jnp.einsum(
            "hqk,khd->hqd",
            weights.astype(jnp.bfloat16),
            block_values,
            preferred_element_type=jnp.float32,
        )
        return ((new_peak, run_total, run_out), None)

    start_carry = (
        jnp.full((head_count, token_count), masked_score, jnp.float32),
        jnp.zeros((head_count, token_count), jnp.float32),
        jnp.zeros((head_count, token_count, HD), jnp.float32),
    )
    (cache_peak, cache_total, cache_out), unused = lax.scan(
        visit, start_carry, (key_blocks, value_blocks)
    )
    global_peak = lax.pmax(cache_peak, "gx")
    fading = jnp.exp(cache_peak - global_peak)
    own_total, own_out = (
        lax.psum_scatter(
            (cache_total * fading).astype(jnp.bfloat16), "gx", scatter_dimension=1, tiled=True
        ).astype(jnp.float32),
        lax.psum_scatter(
            (cache_out * fading[..., None]).astype(jnp.bfloat16),
            "gx",
            scatter_dimension=1,
            tiled=True,
        ).astype(jnp.float32),
    )
    own_peak = lax.dynamic_slice_in_dim(global_peak, first_row, share_rows, 1)
    joint_peak = jnp.maximum(own_peak, recent_peak)
    cache_fade = jnp.exp(own_peak - joint_peak)
    recent_fade = jnp.exp(recent_peak - joint_peak)
    context = (own_out * cache_fade[..., None] + recent_out * recent_fade[..., None]) / (
        own_total * cache_fade + recent_total * recent_fade
    )[..., None]
    context = (
        jnp.transpose(context, (1, 0, 2)).reshape(share_rows, head_count * HD).astype(jnp.bfloat16)
    )
    joined = jnp.concatenate([context, hidden_own], axis=1)
    gathered = lax.all_gather(joined, "gx", axis=0, tiled=True)
    context_cols = context.shape[1]
    row_piece = gathered
    mixed_sum = lax.psum_scatter(
        (
            jnp.dot(row_piece[:, :context_cols], out_weight, preferred_element_type=jnp.float32)
            + jnp.dot(row_piece[:, context_cols:], down_weight, preferred_element_type=jnp.float32)
        ).astype(jnp.bfloat16),
        "gy",
        scatter_dimension=0,
        tiled=True,
    ).astype(jnp.float32)
    return values32 + mixed_sum


def swap(value, axis, bits):
    count = lax.axis_size(axis)
    return lax.ppermute(value, axis, [(d, d ^ bits) for d in range(count)])


def project_body(order_ref, x_ref, w_ref, out_ref):
    out_ref[0] = jnp.dot(x_ref[...], w_ref[...], preferred_element_type=jnp.float32).astype(
        out_ref.dtype
    )


def project(rows, weight, order, width, dtype):
    count = order.shape[0]
    row_count, depth = rows.shape
    return pl.pallas_call(
        project_body,
        out_shape=jax.ShapeDtypeStruct((count, row_count, width), dtype),
        grid_spec=pltpu.PrefetchScalarGridSpec(
            num_scalar_prefetch=1,
            grid=(count,),
            in_specs=[
                pl.BlockSpec((row_count, depth), lambda g, o: (0, 0)),
                pl.BlockSpec((depth, width), lambda g, o: (0, o[g])),
            ],
            out_specs=pl.BlockSpec((1, row_count, width), lambda g, o: (g, 0, 0)),
        ),
        cost_estimate=pl.CostEstimate(
            flops=2 * count * row_count * depth * width,
            bytes_accessed=2 * (row_count * depth + count * depth * width)
            + count * row_count * width * jnp.dtype(dtype).itemsize,
            transcendentals=0,
        ),
        compiler_params=pltpu.CompilerParams(vmem_limit_bytes=24 << 20),
        name="project",
    )(order, rows, weight)


def turn(vectors, cosine, sine_up, sine_down):
    half = ROT // 2
    return (
        vectors * cosine
        + pltpu.roll(vectors, half, 1) * sine_up
        + pltpu.roll(vectors, HD - half, 1) * sine_down
    )


def attend_body(
    sum_a, got_a, sum_b, got_b, tables, keys_old, values_old, per_query, per_new, per_old, out_ref,
    query_s, key_s, value_s,
):
    half_rows = got_a.shape[0]
    scale = HD ** (-0.5)
    for half, (total, got) in enumerate(((sum_a, got_a), (sum_b, got_b))):
        span = pl.ds(half * half_rows, half_rows)
        cosine, up, down = (tables[t, span, :] for t in range(3))
        parts = [
            total[0, :, p * HD : (p + 1) * HD].astype(jnp.float32)
            + got[:, p * HD : (p + 1) * HD].astype(jnp.float32)
            for p in range(3)
        ]
        query_s[span, :] = turn(parts[0], cosine, up, down).astype(jnp.bfloat16)
        key_s[span, :] = turn(parts[1], cosine, up, down).astype(jnp.bfloat16)
        value_s[span, :] = parts[2].astype(jnp.bfloat16)
    tile = 128
    across = (((1,), (1,)), ((), ()))

    def visit(step, unused):
        rows = pl.ds(pl.multiple_of(step * tile, tile), tile)
        query = query_s[rows, :]
        numbers = per_query[rows, :]
        token, first, prefix = numbers[:, 0:1], numbers[:, 1:2], numbers[:, 2:3]
        cached = (
            lax.dot_general(query, keys_old[...], across, preferred_element_type=jnp.float32)
            * scale
        )
        cached = jnp.where(prefix == per_old[...], cached, masked_score)
        recent = (
            lax.dot_general(query, key_s[...], across, preferred_element_type=jnp.float32) * scale
        )
        other = per_new[...]
        recent = jnp.where((other >= first) & (other <= token), recent, masked_score)
        top = jnp.maximum(
            jnp.max(cached, axis=1, keepdims=True), jnp.max(recent, axis=1, keepdims=True)
        )
        cached = jnp.exp(cached - top)
        recent = jnp.exp(recent - top)
        total = jnp.sum(cached, axis=1, keepdims=True) + jnp.sum(recent, axis=1, keepdims=True)
        context = jnp.dot(
            cached.astype(jnp.bfloat16), values_old[...], preferred_element_type=jnp.float32
        ) + jnp.dot(recent.astype(jnp.bfloat16), value_s[...], preferred_element_type=jnp.float32)
        out_ref[rows, :] = (context / total).astype(jnp.bfloat16)
        return unused

    lax.fori_loop(0, query_s.shape[0] // tile, visit, 0)


def attend(sum_a, got_a, sum_b, got_b, tables, keys_old, values_old, per_query, per_new, per_old):
    token_count = per_query.shape[0]
    keys = token_count + keys_old.shape[0]
    return pl.pallas_call(
        attend_body,
        out_shape=jax.ShapeDtypeStruct((token_count, HD), jnp.bfloat16),
        in_specs=[pl.BlockSpec(memory_space=pltpu.VMEM)] * 10,
        out_specs=pl.BlockSpec(memory_space=pltpu.VMEM),
        scratch_shapes=[pltpu.VMEM((token_count, HD), jnp.bfloat16)] * 3,
        cost_estimate=pl.CostEstimate(
            flops=4 * token_count * keys * HD,
            bytes_accessed=4 * token_count * HD * 8,
            transcendentals=token_count * keys,
        ),
        compiler_params=pltpu.CompilerParams(vmem_limit_bytes=32 << 20),
        name="attend",
    )(sum_a, got_a, sum_b, got_b, tables, keys_old, values_old, per_query, per_new, per_old)


def mix_body(order_ref, h0, h1, h2, c0, c1, c2, down_ref, out_w_ref, out_ref):
    width, head = h0.shape[1], c0.shape[1]
    hidden = (h0[...], h1[...], h2[0], h2[1])
    context = (c0[...], c1[...], c2[0], c2[1])
    total = None
    for m in range(4):
        block = order_ref[m]
        down = down_ref[pl.ds(pl.multiple_of(block * width, width), width), :]
        out = out_w_ref[pl.ds(pl.multiple_of(block * head, head), head), :]
        term = jnp.dot(hidden[m], down, preferred_element_type=jnp.float32) + jnp.dot(
            context[m], out, preferred_element_type=jnp.float32
        )
        total = term if total is None else total + term
    out_ref[...] = total.astype(out_ref.dtype)


def mix(order, hidden, context, down_weight, out_weight, dtype):
    rows = hidden[0].shape[0]
    columns = down_weight.shape[1]
    depth = down_weight.shape[0] + out_weight.shape[0]
    return pl.pallas_call(
        mix_body,
        out_shape=jax.ShapeDtypeStruct((rows, columns), dtype),
        in_specs=[pl.BlockSpec(memory_space=pltpu.SMEM)]
        + [pl.BlockSpec(memory_space=pltpu.VMEM)] * 8,
        out_specs=pl.BlockSpec(memory_space=pltpu.VMEM),
        cost_estimate=pl.CostEstimate(
            flops=2 * rows * depth * columns,
            bytes_accessed=2 * (rows * depth + depth * columns + rows * columns),
            transcendentals=0,
        ),
        compiler_params=pltpu.CompilerParams(vmem_limit_bytes=32 << 20),
        name="mix",
    )(order, *hidden, *context, down_weight, out_weight)


def square_shards(
    stream, qkv_weight, up_weight, out_weight, down_weight, cache_keys, cache_values,
    request_prefix, request_lengths, owner_list,
):
    groups = lax.axis_size("gx")
    own = lax.axis_index("gx")
    mine = lax.axis_index("gy")
    local_rows = stream.shape[0]
    feature_count = stream.shape[1] * groups
    token_count = local_rows * lax.axis_size("gy")
    half_rows = token_count // 2
    block_len = cache_keys.shape[0]
    prefix_len = block_len * groups // 2
    head_width = qkv_weight.shape[1] // groups
    hidden_width = up_weight.shape[1] // groups

    values32 = stream.astype(jnp.float32)
    moments = lax.psum((jnp.sum(values32, axis=1), jnp.sum(values32 * values32, axis=1)), "gx")
    average = (moments[0] / feature_count)[:, None]
    square = (moments[1] / feature_count)[:, None]
    normed = ((values32 - average) * lax.rsqrt(square - average * average + epsilon)).astype(
        jnp.bfloat16
    )
    rows_a = jnp.concatenate([normed] + [swap(normed, "gy", 2 * k) for k in range(1, 4)], axis=0)
    rows_b = swap(rows_a, "gy", 1)

    old = jnp.stack([cache_keys, cache_values])
    pieces = []
    for m in range(4):
        piece = lax.dynamic_slice_in_dim(old, (own ^ m) * HD, HD, 2)
        pieces.append(swap(piece, "gx", m) if m else piece)
    old = jnp.concatenate(pieces, axis=1)

    token_ids, segment, offsets, member = token_layout(request_lengths, token_count)
    block = jnp.arange(8, dtype=jnp.int32)
    source = mine ^ (2 * (block % 4) + block // 4)
    token = (
        source[:, None] * local_rows + jnp.arange(local_rows, dtype=jnp.int32)[None, :]
    ).reshape(token_count)
    ending = jnp.cumsum(request_lengths)
    starting = ending - request_lengths
    inside = (token[:, None] >= starting[None, :]) & (token[:, None] < ending[None, :])
    first = jnp.sum(jnp.where(inside, starting[None, :], 0), axis=1)
    prefix = jnp.sum(jnp.where(inside, request_prefix[None, :], 0), axis=1)
    slot = jnp.arange(groups, dtype=jnp.int32)
    order = own ^ slot
    held = jnp.sum(
        jnp.where(
            owner_list[None, :] == order[:, None],
            (slot >= groups // 2).astype(jnp.int32)[None, :],
            0,
        ),
        axis=1,
    )
    per_old = jnp.repeat(held, block_len)[None, :]
    per_new = token[None, :]
    per_query = jnp.stack([token, first, prefix, prefix], axis=1)
    half = ROT // 2
    frequency = rotary_base ** (-2.0 * jnp.arange(half, dtype=jnp.float32) / ROT)
    angles = (token - first + prefix_len).astype(jnp.float32)[:, None] * frequency[None, :]
    cosine, sine = jnp.cos(angles), jnp.sin(angles)
    zero = jnp.zeros_like(sine)
    rest = jnp.zeros((token_count, HD - ROT), jnp.float32)
    tables = jnp.stack(
        [
            jnp.concatenate([cosine, cosine, rest + 1.0], axis=1),
            jnp.concatenate([zero, sine, rest], axis=1),
            jnp.concatenate([-sine, zero, rest], axis=1),
        ]
    )

    def scattered(weight, width):
        send_a = project(rows_a, weight, jnp.stack([own ^ 1, own ^ 3]), width, jnp.bfloat16)
        send_b = project(rows_b, weight, jnp.stack([own ^ 2, own ^ 3]), width, jnp.bfloat16)
        got_a, got_b = swap(send_a, "gx", 1), swap(send_b, "gx", 2)
        keep_a = project(rows_a, weight, jnp.stack([own, own ^ 2]), width, jnp.float32)
        keep_b = project(rows_b, weight, jnp.stack([own, own ^ 1]), width, jnp.float32)
        sum_a, sum_b = keep_a + got_a.astype(jnp.float32), keep_b + got_b.astype(jnp.float32)
        last_a = swap(sum_a[1].astype(jnp.bfloat16), "gx", 2)
        last_b = swap(sum_b[1].astype(jnp.bfloat16), "gx", 1)
        return sum_a, last_a, sum_b, last_b

    def gathered(part_a, part_b):
        one_a, one_b = swap(part_a, "gx", 1), swap(part_b, "gx", 2)
        two_a = swap(jnp.stack([part_a, one_a]), "gx", 2)
        two_b = swap(jnp.stack([part_b, one_b]), "gx", 1)
        return (part_a, one_a, two_a), (part_b, one_b, two_b)

    head = scattered(qkv_weight, head_width)
    sum_a, last_a, sum_b, last_b = scattered(up_weight, hidden_width)
    context = attend(*head, tables, old[0], old[1], per_query, per_new, per_old)
    context_a, context_b = gathered(context[:half_rows], context[half_rows:])
    hidden_a = jax.nn.gelu(sum_a[0] + last_a.astype(jnp.float32), approximate=False)
    hidden_b = jax.nn.gelu(sum_b[0] + last_b.astype(jnp.float32), approximate=False)
    hidden_a, hidden_b = gathered(hidden_a.astype(jnp.bfloat16), hidden_b.astype(jnp.bfloat16))

    order_b = jnp.stack([own, own ^ 2, own ^ 1, own ^ 3])
    mixed_b = mix(order_b, hidden_b, context_b, down_weight, out_weight, jnp.bfloat16)
    other = swap(mixed_b, "gy", 1)
    mixed_a = mix(order, hidden_a, context_a, down_weight, out_weight, jnp.float32)
    mixed = (mixed_a + other.astype(jnp.float32)).reshape(4, local_rows, -1)
    total = values32 + mixed[0]
    for k in range(1, 4):
        total = total + swap(mixed[k].astype(jnp.bfloat16), "gy", 2 * k).astype(jnp.float32)
    return total


def solution(mesh):
    placed = (
        P("gy", "gx"),
        P("gx", "gy"),
        P("gx", "gy"),
        P("gy", "gx"),
        P("gy", "gx"),
        P("gx", "gy"),
        P("gx", "gy"),
        P(),
        P(),
        P(),
    )
    sizes = dict(zip(mesh.axis_names, mesh.devices.shape))

    def program(*arrays):
        heads = arrays[1].shape[1] // (3 * HD) // sizes["gy"]
        square = sizes["gx"] == 4 and sizes["gy"] == 8 and heads == 4
        return jax.shard_map(
            square_shards if square else shards,
            mesh=mesh,
            in_specs=placed,
            out_specs=P("gy", "gx"),
            check_vma=False,
        )(*arrays)

    return program
```

```python
import functools

import jax
import jax.numpy as jnp
from jax import lax
from jax.experimental import pallas as pl
from jax.experimental.pallas import tpu as pltpu
from jax.sharding import PartitionSpec as P

HD = 128
ROT = 32


epsilon = 1e-05
rotary_base = 10000.0
masked_score = -1e30


def token_layout(request_lengths, token_count):
    ending = jnp.cumsum(request_lengths)
    starting = ending - request_lengths
    token_ids = jnp.arange(token_count, dtype=jnp.int32)
    segment = jnp.sum((token_ids[:, None] >= ending[None, :]).astype(jnp.int32), axis=1)
    member = segment[:, None] == jnp.arange(request_lengths.shape[0], dtype=jnp.int32)[None, :]
    first_token = jnp.sum(jnp.where(member, starting[None, :], 0), axis=1)
    return (token_ids, segment, token_ids - first_token, member)


def rotate(vectors, angle_pos):
    halfway = ROT // 2
    frequency = rotary_base ** (-2.0 * jnp.arange(halfway, dtype=jnp.float32) / ROT)
    angles = angle_pos[:, None] * frequency[None, :]
    cosine = jnp.cos(angles)[:, None, :]
    sine_part = jnp.sin(angles)[:, None, :]
    leading = vectors[..., :halfway]
    trailing = vectors[..., halfway:ROT]
    return jnp.concatenate(
        [
            leading * cosine - trailing * sine_part,
            trailing * cosine + leading * sine_part,
            vectors[..., ROT:],
        ],
        axis=-1,
    )


def split_heads(head_block, angle_pos, head_count):
    rows_here = head_block.shape[0]
    head_parts = head_block.reshape(rows_here, head_count, 3, HD)
    queries = rotate(head_parts[:, :, 0], angle_pos).astype(jnp.bfloat16)
    keys_new = rotate(head_parts[:, :, 1], angle_pos).astype(jnp.bfloat16)
    values_new = head_parts[:, :, 2].astype(jnp.bfloat16)
    return (queries, keys_new, values_new)


def shards(
    stream,
    qkv_weight,
    up_weight,
    out_weight,
    down_weight,
    cache_keys,
    cache_values,
    request_prefix,
    request_lengths,
    owner_list,
):
    groups = lax.axis_size("gx")
    group_index = lax.axis_index("gx")
    local_rows = stream.shape[0]
    feature_count = stream.shape[1] * groups
    token_count = local_rows * lax.axis_size("gy")
    share_rows = token_count // groups
    head_cols = qkv_weight.shape[1]
    head_count = head_cols // (3 * HD)
    block_len = cache_keys.shape[0]
    prefix_len = block_len * groups // 2
    score_scale = HD ** (-0.5)
    values32 = stream.astype(jnp.float32)
    moments = lax.psum((jnp.sum(values32, axis=1), jnp.sum(values32 * values32, axis=1)), "gx")
    average = (moments[0] / feature_count)[:, None]
    square = (moments[1] / feature_count)[:, None]
    normed = ((values32 - average) * lax.rsqrt(square - average * average + epsilon)).astype(
        jnp.bfloat16
    )
    row_piece = lax.all_gather(normed, "gy", axis=0, tiled=True)
    partial_sums = jnp.concatenate(
        [
            jnp.dot(row_piece, qkv_weight, preferred_element_type=jnp.float32),
            jnp.dot(row_piece, up_weight, preferred_element_type=jnp.float32),
        ],
        axis=1,
    )
    token_ids, segment, offsets, member = token_layout(request_lengths, token_count)
    angle_pos = (offsets + prefix_len).astype(jnp.float32)
    first_row = group_index * share_rows
    summed = lax.psum_scatter(partial_sums, "gx", scatter_dimension=0, tiled=True)
    up_own = summed[:, head_cols:]
    own_angles = lax.dynamic_slice_in_dim(angle_pos, first_row, share_rows)
    own_query, own_keys, own_values = split_heads(summed[:, :head_cols], own_angles, head_count)
    queries, keys_new, values_new = (
        lax.all_gather(own_query, "gx", axis=0, tiled=True),
        lax.all_gather(own_keys, "gx", axis=0, tiled=True),
        lax.all_gather(own_values, "gx", axis=0, tiled=True),
    )
    hidden_own = jax.nn.gelu(up_own, approximate=False).astype(jnp.bfloat16)
    mine_query = lax.dynamic_slice_in_dim(queries, first_row, share_rows)
    mine_ids = lax.dynamic_slice_in_dim(token_ids, first_row, share_rows)
    mine_segment = lax.dynamic_slice_in_dim(segment, first_row, share_rows)
    visible = (mine_segment[:, None] == segment[None, :]) & (
        token_ids[None, :] <= mine_ids[:, None]
    )
    recent = (
        jnp.einsum("qhd,khd->hqk", mine_query, keys_new, preferred_element_type=jnp.float32)
        * score_scale
    )
    recent = jnp.where(visible[None], recent, masked_score)
    recent_peak = jnp.max(recent, axis=2)
    recent_weights = jnp.exp(recent - recent_peak[..., None])
    recent_total = jnp.sum(recent_weights, axis=2)
    recent_out = jnp.einsum(
        "hqk,khd->hqd",
        recent_weights.astype(jnp.bfloat16),
        values_new,
        preferred_element_type=jnp.float32,
    )
    halfway = groups // 2
    slot_index = jnp.arange(groups, dtype=jnp.int32)
    held_prefix = jnp.sum(
        jnp.where(owner_list == group_index, (slot_index >= halfway).astype(jnp.int32), 0)
    )
    token_prefix = jnp.sum(jnp.where(member, request_prefix[None, :], 0), axis=1)
    active = (token_prefix == held_prefix)[None, :, None]
    step_len = min(512, block_len)
    key_blocks = cache_keys.reshape(block_len // step_len, step_len, head_count, HD)
    value_blocks = cache_values.reshape(block_len // step_len, step_len, head_count, HD)

    def visit(carried, blocks):
        run_peak, run_total, run_out = carried
        block_keys, block_values = blocks
        scores = (
            jnp.einsum("qhd,khd->hqk", queries, block_keys, preferred_element_type=jnp.float32)
            * score_scale
        )
        scores = jnp.where(active, scores, masked_score)
        new_peak = jnp.maximum(run_peak, jnp.max(scores, axis=2))
        fading = jnp.exp(run_peak - new_peak)
        weights = jnp.exp(scores - new_peak[..., None])
        run_total = run_total * fading + jnp.sum(weights, axis=2)
        run_out = run_out * fading[..., None] + jnp.einsum(
            "hqk,khd->hqd",
            weights.astype(jnp.bfloat16),
            block_values,
            preferred_element_type=jnp.float32,
        )
        return ((new_peak, run_total, run_out), None)

    start_carry = (
        jnp.full((head_count, token_count), masked_score, jnp.float32),
        jnp.zeros((head_count, token_count), jnp.float32),
        jnp.zeros((head_count, token_count, HD), jnp.float32),
    )
    (cache_peak, cache_total, cache_out), unused = lax.scan(
        visit, start_carry, (key_blocks, value_blocks)
    )
    global_peak = lax.pmax(cache_peak, "gx")
    fading = jnp.exp(cache_peak - global_peak)
    own_total, own_out = (
        lax.psum_scatter(
            (cache_total * fading).astype(jnp.bfloat16), "gx", scatter_dimension=1, tiled=True
        ).astype(jnp.float32),
        lax.psum_scatter(
            (cache_out * fading[..., None]).astype(jnp.bfloat16),
            "gx",
            scatter_dimension=1,
            tiled=True,
        ).astype(jnp.float32),
    )
    own_peak = lax.dynamic_slice_in_dim(global_peak, first_row, share_rows, 1)
    joint_peak = jnp.maximum(own_peak, recent_peak)
    cache_fade = jnp.exp(own_peak - joint_peak)
    recent_fade = jnp.exp(recent_peak - joint_peak)
    context = (own_out * cache_fade[..., None] + recent_out * recent_fade[..., None]) / (
        own_total * cache_fade + recent_total * recent_fade
    )[..., None]
    context = (
        jnp.transpose(context, (1, 0, 2)).reshape(share_rows, head_count * HD).astype(jnp.bfloat16)
    )
    joined = jnp.concatenate([context, hidden_own], axis=1)
    gathered = lax.all_gather(joined, "gx", axis=0, tiled=True)
    context_cols = context.shape[1]
    row_piece = gathered
    mixed_sum = lax.psum_scatter(
        (
            jnp.dot(row_piece[:, :context_cols], out_weight, preferred_element_type=jnp.float32)
            + jnp.dot(row_piece[:, context_cols:], down_weight, preferred_element_type=jnp.float32)
        ).astype(jnp.bfloat16),
        "gy",
        scatter_dimension=0,
        tiled=True,
    ).astype(jnp.float32)
    return values32 + mixed_sum


CHUNKS = ((0, 1), (1, 2), (2, 4))


def swap(value, axis, bits):
    count = lax.axis_size(axis)
    return lax.ppermute(value, axis, [(d, d ^ bits) for d in range(count)])


def after(value, *others):
    return lax.optimization_barrier((value, *others))[0]


def whole(count):
    return [pl.BlockSpec(memory_space=pltpu.VMEM)] * count


def project_body(plan, widths, row_sets, order_ref, *refs):
    rows, refs = refs[:row_sets], refs[row_sets:]
    weights, outs = refs[: len(widths)], refs[len(widths) :]
    for out, blocks in zip(outs, plan):
        for place, (which, slot) in enumerate(blocks):
            low = 0
            for weight, width in zip(weights, widths):
                start = pl.multiple_of(order_ref[slot] * width, 128)
                out[place, :, low : low + width] = jnp.dot(
                    rows[which][...],
                    weight[:, pl.ds(start, width)],
                    preferred_element_type=jnp.float32,
                ).astype(out.dtype)
                low += width


def project(rows, weights, order, plan, dtype):
    row_count, depth = rows[0].shape
    widths = tuple(w.shape[1] // order.shape[0] for w in weights)
    count = sum(len(blocks) for blocks in plan)
    return pl.pallas_call(
        functools.partial(project_body, plan, widths, len(rows)),
        out_shape=[
            jax.ShapeDtypeStruct((len(blocks), row_count, sum(widths)), dtype) for blocks in plan
        ],
        in_specs=[pl.BlockSpec(memory_space=pltpu.SMEM)] + whole(len(rows) + len(weights)),
        out_specs=whole(len(plan)),
        cost_estimate=pl.CostEstimate(
            flops=2 * count * row_count * depth * sum(widths),
            bytes_accessed=2 * (len(rows) * row_count * depth + count * depth * sum(widths))
            + count * row_count * sum(widths) * jnp.dtype(dtype).itemsize,
            transcendentals=0,
        ),
        compiler_params=pltpu.CompilerParams(vmem_limit_bytes=24 << 20),
        name="project",
    )(order, *rows, *weights)


def turn(vectors, cosine, sine_up, sine_down):
    half = ROT // 2
    return (
        vectors * cosine
        + pltpu.roll(vectors, half, 1) * sine_up
        + pltpu.roll(vectors, HD - half, 1) * sine_down
    )


def attend_body(offsets, tile, *refs):
    count = 2 * len(offsets)
    pairs, refs = refs[:count], refs[count:]
    tables, keys_old, values_old, per_query, per_new, per_old, out_a, out_b = refs[:8]
    query_s, key_s, value_s = refs[8:]
    half_rows = out_a.shape[0]
    scale = HD ** (-0.5)
    for section, offset in enumerate(offsets):
        total, got = pairs[2 * section : 2 * section + 2]
        span = pl.ds(offset, got.shape[0])
        cosine, up, down = (tables[t, span, :] for t in range(3))
        parts = [
            total[0, :, p * HD : (p + 1) * HD] + got[:, p * HD : (p + 1) * HD].astype(jnp.float32)
            for p in range(3)
        ]
        query_s[span, :] = turn(parts[0], cosine, up, down).astype(jnp.bfloat16)
        key_s[span, :] = turn(parts[1], cosine, up, down).astype(jnp.bfloat16)
        value_s[span, :] = parts[2].astype(jnp.bfloat16)
    across = (((1,), (1,)), ((), ()))
    for offset in range(0, 2 * half_rows, tile):
        span = pl.ds(offset, tile)
        query = query_s[span, :]
        numbers = per_query[span, :]
        token, first, prefix = numbers[:, 0:1], numbers[:, 1:2], numbers[:, 2:3]
        cached = (
            lax.dot_general(query, keys_old[...], across, preferred_element_type=jnp.float32)
            * scale
        )
        cached = jnp.where(prefix == per_old[...], cached, masked_score)
        recent = (
            lax.dot_general(query, key_s[...], across, preferred_element_type=jnp.float32) * scale
        )
        other = per_new[...]
        recent = jnp.where((other >= first) & (other <= token), recent, masked_score)
        top = jnp.maximum(
            jnp.max(cached, axis=1, keepdims=True), jnp.max(recent, axis=1, keepdims=True)
        )
        cached = jnp.exp(cached - top)
        recent = jnp.exp(recent - top)
        total = jnp.sum(cached, axis=1, keepdims=True) + jnp.sum(recent, axis=1, keepdims=True)
        context = jnp.dot(
            cached.astype(jnp.bfloat16), values_old[...], preferred_element_type=jnp.float32
        ) + jnp.dot(recent.astype(jnp.bfloat16), value_s[...], preferred_element_type=jnp.float32)
        out = out_a if offset < half_rows else out_b
        out[pl.ds(offset % half_rows, tile), :] = (context / total).astype(jnp.bfloat16)


def attend(offsets, pairs, tables, keys_old, values_old, per_query, per_new, per_old):
    token_count = per_query.shape[0]
    keys = token_count + keys_old.shape[0]
    half = jax.ShapeDtypeStruct((token_count // 2, HD), jnp.bfloat16)
    return pl.pallas_call(
        functools.partial(attend_body, offsets, token_count // 4),
        out_shape=[half, half],
        in_specs=whole(len(pairs) + 6),
        out_specs=whole(2),
        scratch_shapes=[pltpu.VMEM((token_count, HD), jnp.bfloat16)] * 3,
        cost_estimate=pl.CostEstimate(
            flops=4 * token_count * keys * HD,
            bytes_accessed=4 * token_count * HD * 8,
            transcendentals=token_count * keys,
        ),
        compiler_params=pltpu.CompilerParams(vmem_limit_bytes=32 << 20),
        name="attend",
    )(*pairs, tables, keys_old, values_old, per_query, per_new, per_old)


def mix_body(slots, offset, order_ref, h0, h1, h2, c0, c1, c2, down_ref, out_w_ref, out_ref):
    rows, width = h0.shape
    head = c0.shape[1]
    span = pl.ds(offset, rows)
    hidden = (h0[...], h1[...], h2[0], h2[1])
    context = (c0[span, :], c1[span, :], c2[0, span, :], c2[1, span, :])
    total = None
    for m, slot in enumerate(slots):
        block = order_ref[slot]
        down = down_ref[pl.ds(pl.multiple_of(block * width, width), width), :]
        out = out_w_ref[pl.ds(pl.multiple_of(block * head, head), head), :]
        term = jnp.dot(hidden[m], down, preferred_element_type=jnp.float32) + jnp.dot(
            context[m], out, preferred_element_type=jnp.float32
        )
        total = term if total is None else total + term
    out_ref[...] = total.astype(out_ref.dtype)


def mix(order, slots, offset, hidden, context, down_weight, out_weight, dtype):
    rows = hidden[0].shape[0]
    columns = down_weight.shape[1]
    depth = down_weight.shape[0] + out_weight.shape[0]
    return pl.pallas_call(
        functools.partial(mix_body, slots, offset),
        out_shape=jax.ShapeDtypeStruct((rows, columns), dtype),
        in_specs=[pl.BlockSpec(memory_space=pltpu.SMEM)] + whole(8),
        out_specs=pl.BlockSpec(memory_space=pltpu.VMEM),
        cost_estimate=pl.CostEstimate(
            flops=2 * rows * depth * columns,
            bytes_accessed=2 * (rows * depth + depth * columns + rows * columns),
            transcendentals=0,
        ),
        compiler_params=pltpu.CompilerParams(vmem_limit_bytes=32 << 20),
        name="mix",
    )(order, *hidden, *context, down_weight, out_weight)


def square_shards(
    stream, qkv_weight, up_weight, out_weight, down_weight, cache_keys, cache_values,
    request_prefix, request_lengths, owner_list,
):
    groups = lax.axis_size("gx")
    own = lax.axis_index("gx")
    mine = lax.axis_index("gy")
    local_rows = stream.shape[0]
    feature_count = stream.shape[1] * groups
    token_count = local_rows * lax.axis_size("gy")
    block_len = cache_keys.shape[0]
    prefix_len = block_len * groups // 2
    head_width = qkv_weight.shape[1] // groups
    hidden_width = up_weight.shape[1] // groups
    slot = jnp.arange(groups, dtype=jnp.int32)
    order = own ^ slot

    values32 = stream.astype(jnp.float32)
    moments = jnp.stack([jnp.sum(values32, axis=1), jnp.sum(values32 * values32, axis=1)])
    moments = moments + swap(moments, "gx", 1) + (swap(moments, "gx", 2) + swap(moments, "gx", 3))
    moments = moments / feature_count
    average = moments[0][:, None]
    square = moments[1][:, None]
    normed = ((values32 - average) * lax.rsqrt(square - average * average + epsilon)).astype(
        jnp.bfloat16
    )
    near = [normed, swap(normed, "gy", 2), swap(normed, "gy", 4)]
    near.append(swap(near[2], "gy", 2))
    rows = []
    for low, high in CHUNKS:
        rows_a = jnp.concatenate(near[low:high], axis=0) if high - low > 1 else near[low]
        rows.append((rows_a, swap(rows_a, "gy", 1)))

    old = jnp.stack([cache_keys, cache_values])
    pieces = []
    for m in range(4):
        piece = lax.dynamic_slice_in_dim(old, (own ^ m) * HD, HD, 2)
        pieces.append(swap(piece, "gx", m) if m else piece)
    old = jnp.concatenate(pieces, axis=1)

    ending = jnp.cumsum(request_lengths)
    starting = ending - request_lengths
    position = jnp.arange(token_count, dtype=jnp.int32)
    inner, block = position % local_rows, position // local_rows
    token = (mine ^ (2 * (block % 4) + block // 4)) * local_rows + inner
    inside = (token[:, None] >= starting[None, :]) & (token[:, None] < ending[None, :])
    first = jnp.sum(jnp.where(inside, starting[None, :], 0), axis=1)
    prefix = jnp.sum(jnp.where(inside, request_prefix[None, :], 0), axis=1)
    held = jnp.sum(
        jnp.where(
            owner_list[None, :] == order[:, None],
            (slot >= groups // 2).astype(jnp.int32)[None, :],
            0,
        ),
        axis=1,
    )
    per_old = jnp.repeat(held, block_len)[None, :]
    per_new = token[None, :]
    per_query = jnp.stack([token, first, prefix, prefix], axis=1)
    half = ROT // 2
    frequency = rotary_base ** (-2.0 * jnp.arange(half, dtype=jnp.float32) / ROT)
    angles = (token - first + prefix_len).astype(jnp.float32)[:, None] * frequency[None, :]
    cosine, sine = jnp.cos(angles), jnp.sin(angles)
    zero = jnp.zeros_like(sine)
    rest = jnp.zeros((token_count, HD - ROT), jnp.float32)
    tables = jnp.stack(
        [
            jnp.concatenate([cosine, cosine, rest + 1.0], axis=1),
            jnp.concatenate([zero, sine, rest], axis=1),
            jnp.concatenate([-sine, zero, rest], axis=1),
        ]
    )

    sent = []

    def exchange(value_a, value_b, bits_a):
        if len(sent) >= 2:
            value_a, value_b = lax.optimization_barrier((value_a, value_b, sent[-2]))[:2]
        sent.append((swap(value_a, "gx", bits_a), swap(value_b, "gx", 3 - bits_a)))
        return sent[-1]

    class Sums:
        def __init__(self, rows, gate):
            self.rows, self.gate = rows, gate

        def first(self):
            weights = [qkv_weight, up_weight]
            rows_a, rows_b = self.rows
            place = after(order, *self.gate)
            if rows_a.shape[0] == local_rows:
                (part_a,) = project([rows_a], weights, place, [[(0, 1), (0, 3)]], jnp.bfloat16)
                place = after(place, part_a)
                (part_b,) = project([rows_b], weights, place, [[(0, 2), (0, 3)]], jnp.bfloat16)
            else:
                plan = [[(0, 1), (0, 3)], [(1, 2), (1, 3)]]
                part_a, part_b = project([rows_a, rows_b], weights, place, plan, jnp.bfloat16)
            self.got = exchange(part_a, part_b, 1)
            place = after(place, part_b)
            plan = [[(0, 0), (0, 2)], [(1, 0), (1, 1)]]
            self.kept = project([rows_a, rows_b], weights, place, plan, jnp.float32)

        def second(self):
            self.sums = [k + g.astype(jnp.float32) for k, g in zip(self.kept, self.got)]
            self.last = exchange(*(s[1].astype(jnp.bfloat16) for s in self.sums), 2)

    class Parts:
        def __init__(self, part_a, part_b):
            self.own = (part_a, part_b)

        def first(self):
            self.one = exchange(*self.own, 1)

        def second(self):
            self.two = exchange(*(jnp.stack(p) for p in zip(self.own, self.one)), 2)

        def both(self):
            return zip(self.own, self.one, self.two)

    def activated(sums):
        return Parts(
            *(
                jax.nn.gelu(
                    s[0, :, head_width:] + g[:, head_width:].astype(jnp.float32), approximate=False
                ).astype(jnp.bfloat16)
                for s, g in zip(sums.sums, sums.last)
            )
        )

    sums = []
    for r in rows:
        sums.append(Sums(r, sums[-1].kept if sums else ()))
        sums[-1].first()
        if len(sums) > 1:
            sums[-2].second()
        if len(sums) == 3:
            hidden = [activated(sums[0])]
            hidden[0].first()
    sums[2].second()
    hidden.append(activated(sums[1]))
    hidden[1].first()
    hidden.append(activated(sums[2]))
    hidden[2].first()
    offsets, pairs = [], []
    for (low, high), part in zip(CHUNKS, sums):
        for side in range(2):
            offsets.append(side * 4 * local_rows + low * local_rows)
            pairs += [part.sums[side], part.last[side]]
    context = Parts(
        *attend(tuple(offsets), pairs, tables, old[0], old[1], per_query, per_new, per_old)
    )
    context.first()
    hidden[2].second()
    context.second()
    hidden[1].second()
    hidden[0].second()

    total = values32
    context_a, context_b = context.both()
    for index in (2, 1, 0):
        low, high = CHUNKS[index]
        offset = low * local_rows
        hidden_a, hidden_b = hidden[index].both()
        mixed_b = mix(
            order, (0, 2, 1, 3), offset, hidden_b, context_b, down_weight, out_weight, jnp.bfloat16
        )
        other = swap(mixed_b, "gy", 1)
        mixed_a = mix(
            order, (0, 1, 2, 3), offset, hidden_a, context_a, down_weight, out_weight, jnp.float32
        )
        mixed = mixed_a + other.astype(jnp.float32)
        for k in range(low, high):
            part = mixed[(k - low) * local_rows : (k - low + 1) * local_rows]
            if k:
                part = swap(part.astype(jnp.bfloat16), "gy", 2 * k).astype(jnp.float32)
            total = total + part
    return total


def solution(mesh):
    placed = (
        P("gy", "gx"),
        P("gx", "gy"),
        P("gx", "gy"),
        P("gy", "gx"),
        P("gy", "gx"),
        P("gx", "gy"),
        P("gx", "gy"),
        P(),
        P(),
        P(),
    )
    sizes = dict(zip(mesh.axis_names, mesh.devices.shape))

    def program(*arrays):
        heads = arrays[1].shape[1] // (3 * HD) // sizes["gy"]
        square = sizes["gx"] == 4 and sizes["gy"] == 8 and heads == 4
        return jax.shard_map(
            square_shards if square else shards,
            mesh=mesh,
            in_specs=placed,
            out_specs=P("gy", "gx"),
            check_vma=False,
        )(*arrays)

    return program
```

```python
import functools

import jax
import jax.numpy as jnp
import numpy as np
from jax import lax
from jax.experimental import pallas as pl
from jax.experimental.pallas import tpu as pltpu
from jax.sharding import PartitionSpec as P

HD = 128
ROT = 32


epsilon = 1e-05
rotary_base = 10000.0
masked_score = -1e30


def token_layout(request_lengths, token_count):
    ending = jnp.cumsum(request_lengths)
    starting = ending - request_lengths
    token_ids = jnp.arange(token_count, dtype=jnp.int32)
    segment = jnp.sum((token_ids[:, None] >= ending[None, :]).astype(jnp.int32), axis=1)
    member = segment[:, None] == jnp.arange(request_lengths.shape[0], dtype=jnp.int32)[None, :]
    first_token = jnp.sum(jnp.where(member, starting[None, :], 0), axis=1)
    return (token_ids, segment, token_ids - first_token, member)


def rotate(vectors, angle_pos):
    halfway = ROT // 2
    frequency = rotary_base ** (-2.0 * jnp.arange(halfway, dtype=jnp.float32) / ROT)
    angles = angle_pos[:, None] * frequency[None, :]
    cosine = jnp.cos(angles)[:, None, :]
    sine_part = jnp.sin(angles)[:, None, :]
    leading = vectors[..., :halfway]
    trailing = vectors[..., halfway:ROT]
    return jnp.concatenate(
        [
            leading * cosine - trailing * sine_part,
            trailing * cosine + leading * sine_part,
            vectors[..., ROT:],
        ],
        axis=-1,
    )


def split_heads(head_block, angle_pos, head_count):
    rows_here = head_block.shape[0]
    head_parts = head_block.reshape(rows_here, head_count, 3, HD)
    queries = rotate(head_parts[:, :, 0], angle_pos).astype(jnp.bfloat16)
    keys_new = rotate(head_parts[:, :, 1], angle_pos).astype(jnp.bfloat16)
    values_new = head_parts[:, :, 2].astype(jnp.bfloat16)
    return (queries, keys_new, values_new)


def shards(
    stream,
    qkv_weight,
    up_weight,
    out_weight,
    down_weight,
    cache_keys,
    cache_values,
    request_prefix,
    request_lengths,
    owner_list,
):
    groups = lax.axis_size("gx")
    group_index = lax.axis_index("gx")
    local_rows = stream.shape[0]
    feature_count = stream.shape[1] * groups
    token_count = local_rows * lax.axis_size("gy")
    share_rows = token_count // groups
    head_cols = qkv_weight.shape[1]
    head_count = head_cols // (3 * HD)
    block_len = cache_keys.shape[0]
    prefix_len = block_len * groups // 2
    score_scale = HD ** (-0.5)
    values32 = stream.astype(jnp.float32)
    moments = lax.psum((jnp.sum(values32, axis=1), jnp.sum(values32 * values32, axis=1)), "gx")
    average = (moments[0] / feature_count)[:, None]
    square = (moments[1] / feature_count)[:, None]
    normed = ((values32 - average) * lax.rsqrt(square - average * average + epsilon)).astype(
        jnp.bfloat16
    )
    row_piece = lax.all_gather(normed, "gy", axis=0, tiled=True)
    partial_sums = jnp.concatenate(
        [
            jnp.dot(row_piece, qkv_weight, preferred_element_type=jnp.float32),
            jnp.dot(row_piece, up_weight, preferred_element_type=jnp.float32),
        ],
        axis=1,
    )
    token_ids, segment, offsets, member = token_layout(request_lengths, token_count)
    angle_pos = (offsets + prefix_len).astype(jnp.float32)
    first_row = group_index * share_rows
    summed = lax.psum_scatter(partial_sums, "gx", scatter_dimension=0, tiled=True)
    up_own = summed[:, head_cols:]
    own_angles = lax.dynamic_slice_in_dim(angle_pos, first_row, share_rows)
    own_query, own_keys, own_values = split_heads(summed[:, :head_cols], own_angles, head_count)
    queries, keys_new, values_new = (
        lax.all_gather(own_query, "gx", axis=0, tiled=True),
        lax.all_gather(own_keys, "gx", axis=0, tiled=True),
        lax.all_gather(own_values, "gx", axis=0, tiled=True),
    )
    hidden_own = jax.nn.gelu(up_own, approximate=False).astype(jnp.bfloat16)
    mine_query = lax.dynamic_slice_in_dim(queries, first_row, share_rows)
    mine_ids = lax.dynamic_slice_in_dim(token_ids, first_row, share_rows)
    mine_segment = lax.dynamic_slice_in_dim(segment, first_row, share_rows)
    visible = (mine_segment[:, None] == segment[None, :]) & (
        token_ids[None, :] <= mine_ids[:, None]
    )
    recent = (
        jnp.einsum("qhd,khd->hqk", mine_query, keys_new, preferred_element_type=jnp.float32)
        * score_scale
    )
    recent = jnp.where(visible[None], recent, masked_score)
    recent_peak = jnp.max(recent, axis=2)
    recent_weights = jnp.exp(recent - recent_peak[..., None])
    recent_total = jnp.sum(recent_weights, axis=2)
    recent_out = jnp.einsum(
        "hqk,khd->hqd",
        recent_weights.astype(jnp.bfloat16),
        values_new,
        preferred_element_type=jnp.float32,
    )
    halfway = groups // 2
    slot_index = jnp.arange(groups, dtype=jnp.int32)
    held_prefix = jnp.sum(
        jnp.where(owner_list == group_index, (slot_index >= halfway).astype(jnp.int32), 0)
    )
    token_prefix = jnp.sum(jnp.where(member, request_prefix[None, :], 0), axis=1)
    active = (token_prefix == held_prefix)[None, :, None]
    step_len = min(512, block_len)
    key_blocks = cache_keys.reshape(block_len // step_len, step_len, head_count, HD)
    value_blocks = cache_values.reshape(block_len // step_len, step_len, head_count, HD)

    def visit(carried, blocks):
        run_peak, run_total, run_out = carried
        block_keys, block_values = blocks
        scores = (
            jnp.einsum("qhd,khd->hqk", queries, block_keys, preferred_element_type=jnp.float32)
            * score_scale
        )
        scores = jnp.where(active, scores, masked_score)
        new_peak = jnp.maximum(run_peak, jnp.max(scores, axis=2))
        fading = jnp.exp(run_peak - new_peak)
        weights = jnp.exp(scores - new_peak[..., None])
        run_total = run_total * fading + jnp.sum(weights, axis=2)
        run_out = run_out * fading[..., None] + jnp.einsum(
            "hqk,khd->hqd",
            weights.astype(jnp.bfloat16),
            block_values,
            preferred_element_type=jnp.float32,
        )
        return ((new_peak, run_total, run_out), None)

    start_carry = (
        jnp.full((head_count, token_count), masked_score, jnp.float32),
        jnp.zeros((head_count, token_count), jnp.float32),
        jnp.zeros((head_count, token_count, HD), jnp.float32),
    )
    (cache_peak, cache_total, cache_out), unused = lax.scan(
        visit, start_carry, (key_blocks, value_blocks)
    )
    global_peak = lax.pmax(cache_peak, "gx")
    fading = jnp.exp(cache_peak - global_peak)
    own_total, own_out = (
        lax.psum_scatter(
            (cache_total * fading).astype(jnp.bfloat16), "gx", scatter_dimension=1, tiled=True
        ).astype(jnp.float32),
        lax.psum_scatter(
            (cache_out * fading[..., None]).astype(jnp.bfloat16),
            "gx",
            scatter_dimension=1,
            tiled=True,
        ).astype(jnp.float32),
    )
    own_peak = lax.dynamic_slice_in_dim(global_peak, first_row, share_rows, 1)
    joint_peak = jnp.maximum(own_peak, recent_peak)
    cache_fade = jnp.exp(own_peak - joint_peak)
    recent_fade = jnp.exp(recent_peak - joint_peak)
    context = (own_out * cache_fade[..., None] + recent_out * recent_fade[..., None]) / (
        own_total * cache_fade + recent_total * recent_fade
    )[..., None]
    context = (
        jnp.transpose(context, (1, 0, 2)).reshape(share_rows, head_count * HD).astype(jnp.bfloat16)
    )
    joined = jnp.concatenate([context, hidden_own], axis=1)
    gathered = lax.all_gather(joined, "gx", axis=0, tiled=True)
    context_cols = context.shape[1]
    row_piece = gathered
    mixed_sum = lax.psum_scatter(
        (
            jnp.dot(row_piece[:, :context_cols], out_weight, preferred_element_type=jnp.float32)
            + jnp.dot(row_piece[:, context_cols:], down_weight, preferred_element_type=jnp.float32)
        ).astype(jnp.bfloat16),
        "gy",
        scatter_dimension=0,
        tiled=True,
    ).astype(jnp.float32)
    return values32 + mixed_sum


CHUNKS = ((0, 1), (1, 2), (2, 4))


def swap(value, axis, bits):
    count = lax.axis_size(axis)
    return lax.ppermute(value, axis, [(d, d ^ bits) for d in range(count)])


def after(value, *others):
    return lax.optimization_barrier((value, *others))[0]


def whole(count):
    return [pl.BlockSpec(memory_space=pltpu.VMEM)] * count


def local_call(body, name, outs, scalars, arrays, waits=(), flops=0, scratch=()):
    read = len(scalars) + len(arrays)

    def kernel(*refs):
        body(*refs[:read], *refs[read + len(waits) :])

    return pl.pallas_call(
        kernel,
        out_shape=[jax.ShapeDtypeStruct(shape, dtype) for shape, dtype in outs],
        in_specs=[pl.BlockSpec(memory_space=pltpu.SMEM)] * len(scalars)
        + whole(len(arrays))
        + [pl.BlockSpec(memory_space=pl.ANY)] * len(waits),
        out_specs=whole(len(outs)),
        scratch_shapes=scratch,
        cost_estimate=pl.CostEstimate(
            flops=flops,
            bytes_accessed=sum(a.size * a.dtype.itemsize for a in arrays),
            transcendentals=0,
        ),
        compiler_params=pltpu.CompilerParams(vmem_limit_bytes=20 << 20),
        name=name,
    )(*scalars, *arrays, *waits)


def cut_body(info, keys, values, *outs):
    for slot, out in enumerate(outs):
        start = pl.multiple_of((info[0] ^ slot) * HD, HD)
        out[0] = keys[:, pl.ds(start, HD)]
        out[1] = values[:, pl.ds(start, HD)]


def number_body(
    local_rows, prefix_len, block_len, info, frequency, *refs
):
    tables, per_query, per_new, per_old = refs[-4:]
    groups = 4
    requests = (info.shape[0] - 2 - groups) // 2
    blocks = per_query.shape[0] // local_rows
    own, mine = info[0], info[1]
    lane = lax.broadcasted_iota(jnp.int32, (local_rows, HD), 1)
    row = lax.broadcasted_iota(jnp.int32, (local_rows, HD), 0)
    position = lax.broadcasted_iota(jnp.int32, per_new.shape, 1)
    token_row = position
    for block in range(blocks):
        source = mine ^ (2 * (block % 4) + block // 4)
        low = block * local_rows
        inside = (position >= low) & (position < low + local_rows)
        token_row = jnp.where(inside, position + (source * local_rows - low), token_row)
        token = source * local_rows + row
        first = jnp.zeros_like(token)
        prefix = jnp.zeros_like(token)
        start = 0
        for request in range(requests):
            stop = start + info[2 + groups + request]
            inside = (token >= start) & (token < stop)
            first = jnp.where(inside, start, first)
            prefix = jnp.where(inside, info[2 + groups + requests + request], prefix)
            start = stop
        span = pl.ds(low, local_rows)
        per_query[span, :] = jnp.where(lane == 0, token, jnp.where(lane == 1, first, prefix))
        angles = (token - first + prefix_len).astype(jnp.float32) * frequency[...]
        sine = jnp.sin(angles)
        tables[0, span, :] = jnp.where(lane < ROT, jnp.cos(angles), 1.0)
        tables[1, span, :] = jnp.where((lane >= ROT // 2) & (lane < ROT), sine, 0.0)
        tables[2, span, :] = jnp.where(lane < ROT // 2, -sine, 0.0)
    per_new[...] = token_row
    old = lax.broadcasted_iota(jnp.int32, per_old.shape, 1)
    held = jnp.zeros_like(old)
    for m in range(groups):
        second = jnp.int32(0)
        for index in range(groups // 2, groups):
            second = second + jnp.where(info[2 + index] == own ^ m, 1, 0)
        inside = (old >= m * block_len) & (old < (m + 1) * block_len)
        held = jnp.where(inside, second, held)
    per_old[...] = held


def project_body(plan, widths, row_sets, order_ref, *refs):
    rows, refs = refs[:row_sets], refs[row_sets:]
    weights, outs = refs[: len(widths)], refs[len(widths) :]
    for out, blocks in zip(outs, plan):
        for place, (which, slot) in enumerate(blocks):
            low = 0
            for weight, width in zip(weights, widths):
                start = pl.multiple_of(order_ref[slot] * width, 128)
                out[place, :, low : low + width] = jnp.dot(
                    rows[which][...],
                    weight[:, pl.ds(start, width)],
                    preferred_element_type=jnp.float32,
                ).astype(out.dtype)
                low += width


def project(rows, weights, order, plan, dtype):
    row_count, depth = rows[0].shape
    widths = tuple(w.shape[1] // order.shape[0] for w in weights)
    count = sum(len(blocks) for blocks in plan)
    return pl.pallas_call(
        functools.partial(project_body, plan, widths, len(rows)),
        out_shape=[
            jax.ShapeDtypeStruct((len(blocks), row_count, sum(widths)), dtype) for blocks in plan
        ],
        in_specs=[pl.BlockSpec(memory_space=pltpu.SMEM)] + whole(len(rows) + len(weights)),
        out_specs=whole(len(plan)),
        cost_estimate=pl.CostEstimate(
            flops=2 * count * row_count * depth * sum(widths),
            bytes_accessed=2 * (len(rows) * row_count * depth + count * depth * sum(widths))
            + count * row_count * sum(widths) * jnp.dtype(dtype).itemsize,
            transcendentals=0,
        ),
        compiler_params=pltpu.CompilerParams(vmem_limit_bytes=24 << 20),
        name="project",
    )(order, *rows, *weights)


def turn(vectors, cosine, sine_up, sine_down):
    half = ROT // 2
    return (
        vectors * cosine
        + pltpu.roll(vectors, half, 1) * sine_up
        + pltpu.roll(vectors, HD - half, 1) * sine_down
    )


def attend_body(offsets, tile, *refs):
    count = 2 * len(offsets)
    pairs, refs = refs[:count], refs[count:]
    tables, *old, per_query, per_new, per_old, out_a, out_b = refs[:10]
    query_s, key_s, value_s, keys_old, values_old = refs[10:]
    block_len = old[0].shape[1]
    for index, piece in enumerate(old):
        keys_old[index * block_len : (index + 1) * block_len, :] = piece[0]
        values_old[index * block_len : (index + 1) * block_len, :] = piece[1]
    half_rows = out_a.shape[0]
    scale = HD ** (-0.5)
    for section, offset in enumerate(offsets):
        total, got = pairs[2 * section : 2 * section + 2]
        span = pl.ds(offset, got.shape[0])
        cosine, up, down = (tables[t, span, :] for t in range(3))
        parts = [
            total[:, p * HD : (p + 1) * HD] + got[:, p * HD : (p + 1) * HD].astype(jnp.float32)
            for p in range(3)
        ]
        query_s[span, :] = turn(parts[0], cosine, up, down).astype(jnp.bfloat16)
        key_s[span, :] = turn(parts[1], cosine, up, down).astype(jnp.bfloat16)
        value_s[span, :] = parts[2].astype(jnp.bfloat16)
    across = (((1,), (1,)), ((), ()))
    for offset in range(0, 2 * half_rows, tile):
        span = pl.ds(offset, tile)
        query = query_s[span, :]
        numbers = per_query[span, :]
        token, first, prefix = numbers[:, 0:1], numbers[:, 1:2], numbers[:, 2:3]
        cached = (
            lax.dot_general(query, keys_old[...], across, preferred_element_type=jnp.float32)
            * scale
        )
        cached = jnp.where(prefix == per_old[...], cached, masked_score)
        recent = (
            lax.dot_general(query, key_s[...], across, preferred_element_type=jnp.float32) * scale
        )
        other = per_new[...]
        recent = jnp.where((other >= first) & (other <= token), recent, masked_score)
        top = jnp.maximum(
            jnp.max(cached, axis=1, keepdims=True), jnp.max(recent, axis=1, keepdims=True)
        )
        cached = jnp.exp(cached - top)
        recent = jnp.exp(recent - top)
        total = jnp.sum(cached, axis=1, keepdims=True) + jnp.sum(recent, axis=1, keepdims=True)
        context = jnp.dot(
            cached.astype(jnp.bfloat16), values_old[...], preferred_element_type=jnp.float32
        ) + jnp.dot(recent.astype(jnp.bfloat16), value_s[...], preferred_element_type=jnp.float32)
        out = out_a if offset < half_rows else out_b
        out[pl.ds(offset % half_rows, tile), :] = (context / total).astype(jnp.bfloat16)


def attend(offsets, pairs, tables, old, per_query, per_new, per_old, waits):
    token_count = per_query.shape[0]
    keys = token_count + per_old.shape[1]
    return local_call(
        functools.partial(attend_body, offsets, token_count // 4),
        "attend",
        [((token_count // 2, HD), jnp.bfloat16)] * 2,
        [],
        [*pairs, tables, *old, per_query, per_new, per_old],
        waits,
        4 * token_count * keys * HD,
        [pltpu.VMEM((token_count, HD), jnp.bfloat16)] * 3
        + [pltpu.VMEM((per_old.shape[1], HD), jnp.bfloat16)] * 2,
    )


def mix_body(slots, offset, order_ref, h0, h1, h2, c0, c1, c2, down_ref, out_w_ref, out_ref):
    rows, width = h0.shape
    head = c0.shape[1]
    span = pl.ds(offset, rows)
    hidden = (h0[...], h1[...], h2[0], h2[1])
    context = (c0[span, :], c1[span, :], c2[0, span, :], c2[1, span, :])
    total = None
    for m, slot in enumerate(slots):
        block = order_ref[slot]
        down = down_ref[pl.ds(pl.multiple_of(block * width, width), width), :]
        out = out_w_ref[pl.ds(pl.multiple_of(block * head, head), head), :]
        term = jnp.dot(hidden[m], down, preferred_element_type=jnp.float32) + jnp.dot(
            context[m], out, preferred_element_type=jnp.float32
        )
        total = term if total is None else total + term
    out_ref[...] = total.astype(out_ref.dtype)


def mix(order, slots, offset, hidden, context, down_weight, out_weight, dtype):
    rows = hidden[0].shape[0]
    columns = down_weight.shape[1]
    depth = down_weight.shape[0] + out_weight.shape[0]
    return pl.pallas_call(
        functools.partial(mix_body, slots, offset),
        out_shape=jax.ShapeDtypeStruct((rows, columns), dtype),
        in_specs=[pl.BlockSpec(memory_space=pltpu.SMEM)] + whole(8),
        out_specs=pl.BlockSpec(memory_space=pltpu.VMEM),
        cost_estimate=pl.CostEstimate(
            flops=2 * rows * depth * columns,
            bytes_accessed=2 * (rows * depth + depth * columns + rows * columns),
            transcendentals=0,
        ),
        compiler_params=pltpu.CompilerParams(vmem_limit_bytes=32 << 20),
        name="mix",
    )(order, *hidden, *context, down_weight, out_weight)


def square_shards(
    stream, qkv_weight, up_weight, out_weight, down_weight, cache_keys, cache_values,
    request_prefix, request_lengths, owner_list,
):
    groups = lax.axis_size("gx")
    own = lax.axis_index("gx")
    mine = lax.axis_index("gy")
    local_rows = stream.shape[0]
    feature_count = stream.shape[1] * groups
    token_count = local_rows * lax.axis_size("gy")
    block_len = cache_keys.shape[0]
    prefix_len = block_len * groups // 2
    head_width = qkv_weight.shape[1] // groups
    hidden_width = up_weight.shape[1] // groups
    slot = jnp.arange(groups, dtype=jnp.int32)
    order = own ^ slot
    info = jnp.concatenate(
        [jnp.stack([own, mine]), owner_list, request_lengths, request_prefix]
    )

    values32 = stream.astype(jnp.float32)
    moments = jnp.stack([jnp.sum(values32, axis=1), jnp.sum(values32 * values32, axis=1)])
    moments = moments + swap(moments, "gx", 1) + (swap(moments, "gx", 2) + swap(moments, "gx", 3))
    moments = moments / feature_count
    average = moments[0][:, None]
    square = moments[1][:, None]
    normed = ((values32 - average) * lax.rsqrt(square - average * average + epsilon)).astype(
        jnp.bfloat16
    )
    near = [normed, swap(normed, "gy", 2), swap(normed, "gy", 4)]
    near.append(swap(near[2], "gy", 2))
    rows = []
    for low, high in CHUNKS:
        rows_a = jnp.concatenate(near[low:high], axis=0) if high - low > 1 else near[low]
        rows.append((rows_a, swap(rows_a, "gy", 1)))

    outs = [((2, block_len, HD), cache_keys.dtype)] * groups
    old = local_call(cut_body, "cut", outs, [info], [cache_keys, cache_values])
    old = [swap(piece, "gx", m) if m else piece for m, piece in enumerate(old)]

    half = ROT // 2
    frequency = np.zeros((1, HD), np.float32)
    frequency[0, :ROT] = np.tile(rotary_base ** (-2.0 * np.arange(half) / ROT), 2)
    tables, per_query, per_new, per_old = local_call(
        functools.partial(number_body, local_rows, prefix_len, block_len),
        "number",
        [
            ((3, token_count, HD), jnp.float32),
            ((token_count, HD), jnp.int32),
            ((1, token_count), jnp.int32),
            ((1, block_len * groups), jnp.int32),
        ],
        [info],
        [jnp.asarray(frequency)],
    )

    sent = []

    def exchange(value_a, value_b, bits_a):
        if len(sent) >= 2:
            value_a, value_b = lax.optimization_barrier((value_a, value_b, sent[-2]))[:2]
        sent.append((swap(value_a, "gx", bits_a), swap(value_b, "gx", 3 - bits_a)))
        return sent[-1]

    class Sums:
        def __init__(self, rows, gate):
            self.rows, self.gate = rows, gate

        def first(self):
            weights = [qkv_weight, up_weight]
            rows_a, rows_b = self.rows
            place = after(order, *self.gate)
            if rows_a.shape[0] == local_rows:
                (part_a,) = project([rows_a], weights, place, [[(0, 1), (0, 3)]], jnp.bfloat16)
                place = after(place, part_a)
                (part_b,) = project([rows_b], weights, place, [[(0, 2), (0, 3)]], jnp.bfloat16)
            else:
                plan = [[(0, 1), (0, 3)], [(1, 2), (1, 3)]]
                part_a, part_b = project([rows_a, rows_b], weights, place, plan, jnp.bfloat16)
            self.got = exchange(part_a, part_b, 1)
            place = after(place, part_b)
            plan = [[(0, 0), (0, 2)], [(1, 0), (1, 1)]]
            self.kept = project([rows_a, rows_b], weights, place, plan, jnp.float32)

        def second(self):
            self.sums = [k + g.astype(jnp.float32) for k, g in zip(self.kept, self.got)]
            self.last = exchange(*(s[1].astype(jnp.bfloat16) for s in self.sums), 2)

    class Parts:
        def __init__(self, part_a, part_b):
            self.own = (part_a, part_b)

        def first(self):
            self.one = exchange(*self.own, 1)

        def second(self):
            self.two = exchange(*(jnp.stack(p) for p in zip(self.own, self.one)), 2)

        def both(self):
            return zip(self.own, self.one, self.two)

    def activated(sums):
        return Parts(
            *(
                jax.nn.gelu(
                    s[0, :, head_width:] + g[:, head_width:].astype(jnp.float32), approximate=False
                ).astype(jnp.bfloat16)
                for s, g in zip(sums.sums, sums.last)
            )
        )

    sums = []
    for r in rows:
        gate = (*sums[-1].kept, *old[1:]) if len(sums) == 1 else sums[-1].kept if sums else ()
        sums.append(Sums(r, gate))
        sums[-1].first()
        if len(sums) > 1:
            sums[-2].second()
        if len(sums) == 3:
            hidden = [activated(sums[0])]
            hidden[0].first()
    sums[2].second()
    hidden.append(activated(sums[1]))
    hidden[1].first()
    hidden.append(activated(sums[2]))
    hidden[2].first()
    offsets, pairs = [], []
    for (low, high), part in zip(CHUNKS, sums):
        for side in range(2):
            offsets.append(side * 4 * local_rows + low * local_rows)
            pairs += [part.sums[side][0], part.last[side]]
    context = Parts(
        *attend(tuple(offsets), pairs, tables, old, per_query, per_new, per_old, ())
    )
    context.first()
    hidden[2].second()
    context.second()
    hidden[1].second()
    hidden[0].second()

    total = values32
    context_a, context_b = context.both()
    for index in (2, 1, 0):
        low, high = CHUNKS[index]
        offset = low * local_rows
        hidden_a, hidden_b = hidden[index].both()
        mixed_b = mix(
            order, (0, 2, 1, 3), offset, hidden_b, context_b, down_weight, out_weight, jnp.bfloat16
        )
        other = swap(mixed_b, "gy", 1)
        mixed_a = mix(
            order, (0, 1, 2, 3), offset, hidden_a, context_a, down_weight, out_weight, jnp.float32
        )
        mixed = mixed_a + other.astype(jnp.float32)
        for k in range(low, high):
            part = mixed[(k - low) * local_rows : (k - low + 1) * local_rows]
            if k:
                part = swap(part.astype(jnp.bfloat16), "gy", 2 * k).astype(jnp.float32)
            total = total + part
    return total


def solution(mesh):
    placed = (
        P("gy", "gx"),
        P("gx", "gy"),
        P("gx", "gy"),
        P("gy", "gx"),
        P("gy", "gx"),
        P("gx", "gy"),
        P("gx", "gy"),
        P(),
        P(),
        P(),
    )
    sizes = dict(zip(mesh.axis_names, mesh.devices.shape))

    def program(*arrays):
        heads = arrays[1].shape[1] // (3 * HD) // sizes["gy"]
        square = sizes["gx"] == 4 and sizes["gy"] == 8 and heads == 4
        return jax.shard_map(
            square_shards if square else shards,
            mesh=mesh,
            in_specs=placed,
            out_specs=P("gy", "gx"),
            check_vma=False,
        )(*arrays)

    return program
```

```python
import functools

import jax
import jax.numpy as jnp
import numpy as np
from jax import lax
from jax.experimental import pallas as pl
from jax.experimental.pallas import tpu as pltpu
from jax.sharding import PartitionSpec as P

HD = 128
ROT = 32


epsilon = 1e-05
rotary_base = 10000.0
masked_score = -1e30


def token_layout(request_lengths, token_count):
    ending = jnp.cumsum(request_lengths)
    starting = ending - request_lengths
    token_ids = jnp.arange(token_count, dtype=jnp.int32)
    segment = jnp.sum((token_ids[:, None] >= ending[None, :]).astype(jnp.int32), axis=1)
    member = segment[:, None] == jnp.arange(request_lengths.shape[0], dtype=jnp.int32)[None, :]
    first_token = jnp.sum(jnp.where(member, starting[None, :], 0), axis=1)
    return (token_ids, segment, token_ids - first_token, member)


def rotate(vectors, angle_pos):
    halfway = ROT // 2
    frequency = rotary_base ** (-2.0 * jnp.arange(halfway, dtype=jnp.float32) / ROT)
    angles = angle_pos[:, None] * frequency[None, :]
    cosine = jnp.cos(angles)[:, None, :]
    sine_part = jnp.sin(angles)[:, None, :]
    leading = vectors[..., :halfway]
    trailing = vectors[..., halfway:ROT]
    return jnp.concatenate(
        [
            leading * cosine - trailing * sine_part,
            trailing * cosine + leading * sine_part,
            vectors[..., ROT:],
        ],
        axis=-1,
    )


def split_heads(head_block, angle_pos, head_count):
    rows_here = head_block.shape[0]
    head_parts = head_block.reshape(rows_here, head_count, 3, HD)
    queries = rotate(head_parts[:, :, 0], angle_pos).astype(jnp.bfloat16)
    keys_new = rotate(head_parts[:, :, 1], angle_pos).astype(jnp.bfloat16)
    values_new = head_parts[:, :, 2].astype(jnp.bfloat16)
    return (queries, keys_new, values_new)


def shards(
    stream,
    qkv_weight,
    up_weight,
    out_weight,
    down_weight,
    cache_keys,
    cache_values,
    request_prefix,
    request_lengths,
    owner_list,
):
    groups = lax.axis_size("gx")
    group_index = lax.axis_index("gx")
    local_rows = stream.shape[0]
    feature_count = stream.shape[1] * groups
    token_count = local_rows * lax.axis_size("gy")
    share_rows = token_count // groups
    head_cols = qkv_weight.shape[1]
    head_count = head_cols // (3 * HD)
    block_len = cache_keys.shape[0]
    prefix_len = block_len * groups // 2
    score_scale = HD ** (-0.5)
    values32 = stream.astype(jnp.float32)
    moments = lax.psum((jnp.sum(values32, axis=1), jnp.sum(values32 * values32, axis=1)), "gx")
    average = (moments[0] / feature_count)[:, None]
    square = (moments[1] / feature_count)[:, None]
    normed = ((values32 - average) * lax.rsqrt(square - average * average + epsilon)).astype(
        jnp.bfloat16
    )
    row_piece = lax.all_gather(normed, "gy", axis=0, tiled=True)
    partial_sums = jnp.concatenate(
        [
            jnp.dot(row_piece, qkv_weight, preferred_element_type=jnp.float32),
            jnp.dot(row_piece, up_weight, preferred_element_type=jnp.float32),
        ],
        axis=1,
    )
    token_ids, segment, offsets, member = token_layout(request_lengths, token_count)
    angle_pos = (offsets + prefix_len).astype(jnp.float32)
    first_row = group_index * share_rows
    summed = lax.psum_scatter(partial_sums, "gx", scatter_dimension=0, tiled=True)
    up_own = summed[:, head_cols:]
    own_angles = lax.dynamic_slice_in_dim(angle_pos, first_row, share_rows)
    own_query, own_keys, own_values = split_heads(summed[:, :head_cols], own_angles, head_count)
    queries, keys_new, values_new = (
        lax.all_gather(own_query, "gx", axis=0, tiled=True),
        lax.all_gather(own_keys, "gx", axis=0, tiled=True),
        lax.all_gather(own_values, "gx", axis=0, tiled=True),
    )
    hidden_own = jax.nn.gelu(up_own, approximate=False).astype(jnp.bfloat16)
    mine_query = lax.dynamic_slice_in_dim(queries, first_row, share_rows)
    mine_ids = lax.dynamic_slice_in_dim(token_ids, first_row, share_rows)
    mine_segment = lax.dynamic_slice_in_dim(segment, first_row, share_rows)
    visible = (mine_segment[:, None] == segment[None, :]) & (
        token_ids[None, :] <= mine_ids[:, None]
    )
    recent = (
        jnp.einsum("qhd,khd->hqk", mine_query, keys_new, preferred_element_type=jnp.float32)
        * score_scale
    )
    recent = jnp.where(visible[None], recent, masked_score)
    recent_peak = jnp.max(recent, axis=2)
    recent_weights = jnp.exp(recent - recent_peak[..., None])
    recent_total = jnp.sum(recent_weights, axis=2)
    recent_out = jnp.einsum(
        "hqk,khd->hqd",
        recent_weights.astype(jnp.bfloat16),
        values_new,
        preferred_element_type=jnp.float32,
    )
    halfway = groups // 2
    slot_index = jnp.arange(groups, dtype=jnp.int32)
    held_prefix = jnp.sum(
        jnp.where(owner_list == group_index, (slot_index >= halfway).astype(jnp.int32), 0)
    )
    token_prefix = jnp.sum(jnp.where(member, request_prefix[None, :], 0), axis=1)
    active = (token_prefix == held_prefix)[None, :, None]
    step_len = min(512, block_len)
    key_blocks = cache_keys.reshape(block_len // step_len, step_len, head_count, HD)
    value_blocks = cache_values.reshape(block_len // step_len, step_len, head_count, HD)

    def visit(carried, blocks):
        run_peak, run_total, run_out = carried
        block_keys, block_values = blocks
        scores = (
            jnp.einsum("qhd,khd->hqk", queries, block_keys, preferred_element_type=jnp.float32)
            * score_scale
        )
        scores = jnp.where(active, scores, masked_score)
        new_peak = jnp.maximum(run_peak, jnp.max(scores, axis=2))
        fading = jnp.exp(run_peak - new_peak)
        weights = jnp.exp(scores - new_peak[..., None])
        run_total = run_total * fading + jnp.sum(weights, axis=2)
        run_out = run_out * fading[..., None] + jnp.einsum(
            "hqk,khd->hqd",
            weights.astype(jnp.bfloat16),
            block_values,
            preferred_element_type=jnp.float32,
        )
        return ((new_peak, run_total, run_out), None)

    start_carry = (
        jnp.full((head_count, token_count), masked_score, jnp.float32),
        jnp.zeros((head_count, token_count), jnp.float32),
        jnp.zeros((head_count, token_count, HD), jnp.float32),
    )
    (cache_peak, cache_total, cache_out), unused = lax.scan(
        visit, start_carry, (key_blocks, value_blocks)
    )
    global_peak = lax.pmax(cache_peak, "gx")
    fading = jnp.exp(cache_peak - global_peak)
    own_total, own_out = (
        lax.psum_scatter(
            (cache_total * fading).astype(jnp.bfloat16), "gx", scatter_dimension=1, tiled=True
        ).astype(jnp.float32),
        lax.psum_scatter(
            (cache_out * fading[..., None]).astype(jnp.bfloat16),
            "gx",
            scatter_dimension=1,
            tiled=True,
        ).astype(jnp.float32),
    )
    own_peak = lax.dynamic_slice_in_dim(global_peak, first_row, share_rows, 1)
    joint_peak = jnp.maximum(own_peak, recent_peak)
    cache_fade = jnp.exp(own_peak - joint_peak)
    recent_fade = jnp.exp(recent_peak - joint_peak)
    context = (own_out * cache_fade[..., None] + recent_out * recent_fade[..., None]) / (
        own_total * cache_fade + recent_total * recent_fade
    )[..., None]
    context = (
        jnp.transpose(context, (1, 0, 2)).reshape(share_rows, head_count * HD).astype(jnp.bfloat16)
    )
    joined = jnp.concatenate([context, hidden_own], axis=1)
    gathered = lax.all_gather(joined, "gx", axis=0, tiled=True)
    context_cols = context.shape[1]
    row_piece = gathered
    mixed_sum = lax.psum_scatter(
        (
            jnp.dot(row_piece[:, :context_cols], out_weight, preferred_element_type=jnp.float32)
            + jnp.dot(row_piece[:, context_cols:], down_weight, preferred_element_type=jnp.float32)
        ).astype(jnp.bfloat16),
        "gy",
        scatter_dimension=0,
        tiled=True,
    ).astype(jnp.float32)
    return values32 + mixed_sum


CHUNKS = ((0, 1), (1, 2), (2, 4))


def swap(value, axis, bits):
    count = lax.axis_size(axis)
    return lax.ppermute(value, axis, [(d, d ^ bits) for d in range(count)])


def after(value, *others):
    return lax.optimization_barrier((value, *others))[0]


def whole(count):
    return [pl.BlockSpec(memory_space=pltpu.VMEM)] * count


def local_call(body, name, outs, scalars, arrays, waits=(), flops=0, scratch=()):
    read = len(scalars) + len(arrays)

    def kernel(*refs):
        body(*refs[:read], *refs[read + len(waits) :])

    return pl.pallas_call(
        kernel,
        out_shape=[jax.ShapeDtypeStruct(shape, dtype) for shape, dtype in outs],
        in_specs=[pl.BlockSpec(memory_space=pltpu.SMEM)] * len(scalars)
        + whole(len(arrays))
        + [pl.BlockSpec(memory_space=pl.ANY)] * len(waits),
        out_specs=whole(len(outs)),
        scratch_shapes=scratch,
        cost_estimate=pl.CostEstimate(
            flops=flops,
            bytes_accessed=sum(a.size * a.dtype.itemsize for a in arrays),
            transcendentals=0,
        ),
        compiler_params=pltpu.CompilerParams(vmem_limit_bytes=20 << 20),
        name=name,
    )(*scalars, *arrays, *waits)


def cut_body(info, keys, values, *outs):
    for slot, out in enumerate(outs):
        start = pl.multiple_of((info[0] ^ slot) * HD, HD)
        out[0] = keys[:, pl.ds(start, HD)]
        out[1] = values[:, pl.ds(start, HD)]


def number_body(
    local_rows, prefix_len, block_len, info, frequency, *refs
):
    tables, per_query, per_new, per_old = refs[-4:]
    groups = 4
    requests = (info.shape[0] - 2 - groups) // 2
    blocks = per_query.shape[0] // local_rows
    own, mine = info[0], info[1]
    lane = lax.broadcasted_iota(jnp.int32, (local_rows, HD), 1)
    row = lax.broadcasted_iota(jnp.int32, (local_rows, HD), 0)
    position = lax.broadcasted_iota(jnp.int32, per_new.shape, 1)
    token_row = position
    for block in range(blocks):
        source = mine ^ (2 * (block % 4) + block // 4)
        low = block * local_rows
        inside = (position >= low) & (position < low + local_rows)
        token_row = jnp.where(inside, position + (source * local_rows - low), token_row)
        token = source * local_rows + row
        first = jnp.zeros_like(token)
        prefix = jnp.zeros_like(token)
        start = 0
        for request in range(requests):
            stop = start + info[2 + groups + request]
            inside = (token >= start) & (token < stop)
            first = jnp.where(inside, start, first)
            prefix = jnp.where(inside, info[2 + groups + requests + request], prefix)
            start = stop
        span = pl.ds(low, local_rows)
        per_query[span, :] = jnp.where(lane == 0, token, jnp.where(lane == 1, first, prefix))
        angles = (token - first + prefix_len).astype(jnp.float32) * frequency[...]
        sine = jnp.sin(angles)
        tables[0, span, :] = jnp.where(lane < ROT, jnp.cos(angles), 1.0)
        tables[1, span, :] = jnp.where((lane >= ROT // 2) & (lane < ROT), sine, 0.0)
        tables[2, span, :] = jnp.where(lane < ROT // 2, -sine, 0.0)
    per_new[...] = token_row
    old = lax.broadcasted_iota(jnp.int32, per_old.shape, 1)
    held = jnp.zeros_like(old)
    for m in range(groups):
        second = jnp.int32(0)
        for index in range(groups // 2, groups):
            second = second + jnp.where(info[2 + index] == own ^ m, 1, 0)
        inside = (old >= m * block_len) & (old < (m + 1) * block_len)
        held = jnp.where(inside, second, held)
    per_old[...] = held


def project_body(plan, widths, row_sets, order_ref, *refs):
    rows, refs = refs[:row_sets], refs[row_sets:]
    weights, outs = refs[: len(widths)], refs[len(widths) :]
    for out, blocks in zip(outs, plan):
        for place, (which, slot) in enumerate(blocks):
            low = 0
            for weight, width in zip(weights, widths):
                start = pl.multiple_of(order_ref[slot] * width, 128)
                out[place, :, low : low + width] = jnp.dot(
                    rows[which][...],
                    weight[:, pl.ds(start, width)],
                    preferred_element_type=jnp.float32,
                ).astype(out.dtype)
                low += width


def project(rows, weights, order, plan, dtype):
    row_count, depth = rows[0].shape
    widths = tuple(w.shape[1] // order.shape[0] for w in weights)
    count = sum(len(blocks) for blocks in plan)
    return pl.pallas_call(
        functools.partial(project_body, plan, widths, len(rows)),
        out_shape=[
            jax.ShapeDtypeStruct((len(blocks), row_count, sum(widths)), dtype) for blocks in plan
        ],
        in_specs=[pl.BlockSpec(memory_space=pltpu.SMEM)] + whole(len(rows) + len(weights)),
        out_specs=whole(len(plan)),
        cost_estimate=pl.CostEstimate(
            flops=2 * count * row_count * depth * sum(widths),
            bytes_accessed=2 * (len(rows) * row_count * depth + count * depth * sum(widths))
            + count * row_count * sum(widths) * jnp.dtype(dtype).itemsize,
            transcendentals=0,
        ),
        compiler_params=pltpu.CompilerParams(vmem_limit_bytes=24 << 20),
        name="project",
    )(order, *rows, *weights)


def turn(vectors, cosine, sine_up, sine_down):
    half = ROT // 2
    return (
        vectors * cosine
        + pltpu.roll(vectors, half, 1) * sine_up
        + pltpu.roll(vectors, HD - half, 1) * sine_down
    )


def attend_body(offsets, tile, *refs):
    count = 2 * len(offsets)
    pairs, refs = refs[:count], refs[count:]
    tables, *old, per_query, per_new, per_old, out_a, out_b = refs[:10]
    query_s, key_s, value_s, keys_old, values_old = refs[10:]
    block_len = old[0].shape[1]
    for index, piece in enumerate(old):
        keys_old[index * block_len : (index + 1) * block_len, :] = piece[0]
        values_old[index * block_len : (index + 1) * block_len, :] = piece[1]
    half_rows = out_a.shape[0]
    scale = HD ** (-0.5)
    for section, offset in enumerate(offsets):
        total, got = pairs[2 * section : 2 * section + 2]
        span = pl.ds(offset, got.shape[0])
        cosine, up, down = (tables[t, span, :] for t in range(3))
        parts = [
            total[:, p * HD : (p + 1) * HD] + got[:, p * HD : (p + 1) * HD].astype(jnp.float32)
            for p in range(3)
        ]
        query_s[span, :] = turn(parts[0], cosine, up, down).astype(jnp.bfloat16)
        key_s[span, :] = turn(parts[1], cosine, up, down).astype(jnp.bfloat16)
        value_s[span, :] = parts[2].astype(jnp.bfloat16)
    across = (((1,), (1,)), ((), ()))
    for offset in range(0, 2 * half_rows, tile):
        span = pl.ds(offset, tile)
        query = query_s[span, :]
        numbers = per_query[span, :]
        token, first, prefix = numbers[:, 0:1], numbers[:, 1:2], numbers[:, 2:3]
        cached = (
            lax.dot_general(query, keys_old[...], across, preferred_element_type=jnp.float32)
            * scale
        )
        cached = jnp.where(prefix == per_old[...], cached, masked_score)
        recent = (
            lax.dot_general(query, key_s[...], across, preferred_element_type=jnp.float32) * scale
        )
        other = per_new[...]
        recent = jnp.where((other >= first) & (other <= token), recent, masked_score)
        top = jnp.maximum(
            jnp.max(cached, axis=1, keepdims=True), jnp.max(recent, axis=1, keepdims=True)
        )
        cached = jnp.exp(cached - top)
        recent = jnp.exp(recent - top)
        total = jnp.sum(cached, axis=1, keepdims=True) + jnp.sum(recent, axis=1, keepdims=True)
        context = jnp.dot(
            cached.astype(jnp.bfloat16), values_old[...], preferred_element_type=jnp.float32
        ) + jnp.dot(recent.astype(jnp.bfloat16), value_s[...], preferred_element_type=jnp.float32)
        out = out_a if offset < half_rows else out_b
        out[pl.ds(offset % half_rows, tile), :] = (context / total).astype(jnp.bfloat16)


def attend(offsets, pairs, tables, old, per_query, per_new, per_old, waits):
    token_count = per_query.shape[0]
    keys = token_count + per_old.shape[1]
    return local_call(
        functools.partial(attend_body, offsets, token_count // 4),
        "attend",
        [((token_count // 2, HD), jnp.bfloat16)] * 2,
        [],
        [*pairs, tables, *old, per_query, per_new, per_old],
        waits,
        4 * token_count * keys * HD,
        [pltpu.VMEM((token_count, HD), jnp.bfloat16)] * 3
        + [pltpu.VMEM((per_old.shape[1], HD), jnp.bfloat16)] * 2,
    )


def mix_body(offset, info, *refs):
    down_ref, out_w_ref, out_a, out_b = refs[-4:]
    for side, slots, out_ref in ((1, (0, 2, 1, 3), out_b), (0, (0, 1, 2, 3), out_a)):
        h0, h1, h2, c0, c1, c2 = refs[6 * side : 6 * side + 6]
        rows, width = h0.shape
        head = c0.shape[1]
        span = pl.ds(offset, rows)
        hidden = (h0[...], h1[...], h2[0], h2[1])
        context = (c0[span, :], c1[span, :], c2[0, span, :], c2[1, span, :])
        total = None
        for m, slot in enumerate(slots):
            block = info[0] ^ slot
            down = down_ref[pl.ds(pl.multiple_of(block * width, width), width), :]
            out = out_w_ref[pl.ds(pl.multiple_of(block * head, head), head), :]
            term = jnp.dot(hidden[m], down, preferred_element_type=jnp.float32) + jnp.dot(
                context[m], out, preferred_element_type=jnp.float32
            )
            total = term if total is None else total + term
        out_ref[...] = total.astype(out_ref.dtype)


def mix(info, offset, hidden, context, weights, waits):
    rows, columns = hidden[0][0].shape[0], weights[0].shape[1]
    depth = sum(w.shape[0] for w in weights)
    arrays = [a for side in range(2) for a in (*hidden[side], *context[side])]
    return local_call(
        functools.partial(mix_body, offset),
        "mix",
        [((rows, columns), jnp.float32), ((rows, columns), jnp.bfloat16)],
        [info],
        [*arrays, *weights],
        waits,
        4 * rows * depth * columns,
    )


def merge_body(mixed, other, *outs):
    rows = outs[0].shape[0]
    for index, out in enumerate(outs):
        span = pl.ds(index * rows, rows)
        out[...] = (mixed[span, :] + other[span, :].astype(jnp.float32)).astype(out.dtype)


def merge(mixed, other, count, first, waits):
    shape = (mixed.shape[0] // count, mixed.shape[1])
    outs = [(shape, other.dtype)] * count
    if first:
        outs[0] = shape, jnp.float32
    return local_call(merge_body, "merge", outs, [], [mixed, other], waits)


def square_shards(
    stream, qkv_weight, up_weight, out_weight, down_weight, cache_keys, cache_values,
    request_prefix, request_lengths, owner_list,
):
    groups = lax.axis_size("gx")
    own = lax.axis_index("gx")
    mine = lax.axis_index("gy")
    local_rows = stream.shape[0]
    feature_count = stream.shape[1] * groups
    token_count = local_rows * lax.axis_size("gy")
    block_len = cache_keys.shape[0]
    prefix_len = block_len * groups // 2
    head_width = qkv_weight.shape[1] // groups
    hidden_width = up_weight.shape[1] // groups
    slot = jnp.arange(groups, dtype=jnp.int32)
    order = own ^ slot
    info = jnp.concatenate(
        [jnp.stack([own, mine]), owner_list, request_lengths, request_prefix]
    )

    values32 = stream.astype(jnp.float32)
    moments = jnp.stack([jnp.sum(values32, axis=1), jnp.sum(values32 * values32, axis=1)])
    moments = moments + swap(moments, "gx", 1) + (swap(moments, "gx", 2) + swap(moments, "gx", 3))
    moments = moments / feature_count
    average = moments[0][:, None]
    square = moments[1][:, None]
    normed = ((values32 - average) * lax.rsqrt(square - average * average + epsilon)).astype(
        jnp.bfloat16
    )
    near = [normed, swap(normed, "gy", 2), swap(normed, "gy", 4)]
    near.append(swap(near[2], "gy", 2))
    rows = []
    for low, high in CHUNKS:
        rows_a = jnp.concatenate(near[low:high], axis=0) if high - low > 1 else near[low]
        rows.append((rows_a, swap(rows_a, "gy", 1)))

    outs = [((2, block_len, HD), cache_keys.dtype)] * groups
    old = local_call(cut_body, "cut", outs, [info], [cache_keys, cache_values])
    old = [swap(piece, "gx", m) if m else piece for m, piece in enumerate(old)]

    half = ROT // 2
    frequency = np.zeros((1, HD), np.float32)
    frequency[0, :ROT] = np.tile(rotary_base ** (-2.0 * np.arange(half) / ROT), 2)
    tables, per_query, per_new, per_old = local_call(
        functools.partial(number_body, local_rows, prefix_len, block_len),
        "number",
        [
            ((3, token_count, HD), jnp.float32),
            ((token_count, HD), jnp.int32),
            ((1, token_count), jnp.int32),
            ((1, block_len * groups), jnp.int32),
        ],
        [info],
        [jnp.asarray(frequency)],
    )

    sent = []

    def exchange(value_a, value_b, bits_a):
        if len(sent) >= 2:
            value_a, value_b = lax.optimization_barrier((value_a, value_b, sent[-2]))[:2]
        sent.append((swap(value_a, "gx", bits_a), swap(value_b, "gx", 3 - bits_a)))
        return sent[-1]

    class Sums:
        def __init__(self, rows, gate):
            self.rows, self.gate = rows, gate

        def first(self):
            weights = [qkv_weight, up_weight]
            rows_a, rows_b = self.rows
            place = after(order, *self.gate)
            if rows_a.shape[0] == local_rows:
                (part_a,) = project([rows_a], weights, place, [[(0, 1), (0, 3)]], jnp.bfloat16)
                place = after(place, part_a)
                (part_b,) = project([rows_b], weights, place, [[(0, 2), (0, 3)]], jnp.bfloat16)
            else:
                plan = [[(0, 1), (0, 3)], [(1, 2), (1, 3)]]
                part_a, part_b = project([rows_a, rows_b], weights, place, plan, jnp.bfloat16)
            self.got = exchange(part_a, part_b, 1)
            place = after(place, part_b)
            plan = [[(0, 0), (0, 2)], [(1, 0), (1, 1)]]
            self.kept = project([rows_a, rows_b], weights, place, plan, jnp.float32)

        def second(self):
            self.sums = [k + g.astype(jnp.float32) for k, g in zip(self.kept, self.got)]
            self.last = exchange(*(s[1].astype(jnp.bfloat16) for s in self.sums), 2)

    class Parts:
        def __init__(self, part_a, part_b):
            self.own = (part_a, part_b)

        def first(self):
            self.one = exchange(*self.own, 1)

        def second(self):
            self.two = exchange(*(jnp.stack(p) for p in zip(self.own, self.one)), 2)

        def both(self):
            return zip(self.own, self.one, self.two)

    def activated(sums):
        return Parts(
            *(
                jax.nn.gelu(
                    s[0, :, head_width:] + g[:, head_width:].astype(jnp.float32), approximate=False
                ).astype(jnp.bfloat16)
                for s, g in zip(sums.sums, sums.last)
            )
        )

    sums = []
    for r in rows:
        gate = (*sums[-1].kept, *old[1:]) if len(sums) == 1 else sums[-1].kept if sums else ()
        sums.append(Sums(r, gate))
        sums[-1].first()
        if len(sums) > 1:
            sums[-2].second()
        if len(sums) == 3:
            hidden = [activated(sums[0])]
            hidden[0].first()
    sums[2].second()
    hidden.append(activated(sums[1]))
    hidden[1].first()
    hidden.append(activated(sums[2]))
    hidden[2].first()
    offsets, pairs = [], []
    for (low, high), part in zip(CHUNKS, sums):
        for side in range(2):
            offsets.append(side * 4 * local_rows + low * local_rows)
            pairs += [part.sums[side][0], part.last[side]]
    context = Parts(
        *attend(tuple(offsets), pairs, tables, old, per_query, per_new, per_old, ())
    )
    context.first()
    hidden[2].second()
    context.second()
    hidden[1].second()
    hidden[0].second()

    total = values32
    context_c = tuple(context.both())
    last = ()
    for index in (2, 1, 0):
        low, high = CHUNKS[index]
        hidden_c = tuple(hidden[index].both())
        weights = [down_weight, out_weight]
        mixed_a, mixed_b = mix(info, low * local_rows, hidden_c, context_c, weights, last)
        other = swap(mixed_b, "gy", 1)
        parts = merge(mixed_a, other, high - low, low == 0, ())
        last = (mixed_b,)
        for k in range(low, high):
            part = parts[k - low]
            if k:
                part = swap(part, "gy", 2 * k).astype(jnp.float32)
            total = total + part
    return total


def solution(mesh):
    placed = (
        P("gy", "gx"),
        P("gx", "gy"),
        P("gx", "gy"),
        P("gy", "gx"),
        P("gy", "gx"),
        P("gx", "gy"),
        P("gx", "gy"),
        P(),
        P(),
        P(),
    )
    sizes = dict(zip(mesh.axis_names, mesh.devices.shape))

    def program(*arrays):
        heads = arrays[1].shape[1] // (3 * HD) // sizes["gy"]
        square = sizes["gx"] == 4 and sizes["gy"] == 8 and heads == 4
        return jax.shard_map(
            square_shards if square else shards,
            mesh=mesh,
            in_specs=placed,
            out_specs=P("gy", "gx"),
            check_vma=False,
        )(*arrays)

    return program
```
